32 devices in a mesh: groups: 2 (over y), pix: 8 (over z, x), dp: 2 (over core).
Axes of the slice: x: 2, y: 2, z: 4, core: 2. Of those that a mesh axis runs over, the one named last changes fastest.
Arguments:
- features: bfloat16 [64, 64, 512], P('pix', None, ('groups', 'dp')), parts along dimension 2, may hold values from -6 to 6
- cheb_weights: bfloat16 [4, 64, 64], replicated, may hold values from -0.375 to 0.375
- out_bias: float32 [64], replicated, may hold values from -3 to 3
- lap_tiles: bfloat16 [64, 64, 576], P('pix'), as said below
- neighbours: int32 [64, 2], P('pix'), may hold values from 0 to 15, as said below
- send_blocks: int32 [8, 4, 2], P('pix'), may hold values from 0 to 7, as said below
- pixel_mask: int32 [64, 64], P('pix'), may hold values 0 or 1
- cotangent: bfloat16 [64, 64, 512], P('pix', None, ('groups', 'dp')), parts along dimension 2, may hold values from -6 to 6
Outputs:
- output_maps: bfloat16 [64, 64, 512], P('pix', None, ('groups', 'dp')), parts along dimension 2
- grad_features: bfloat16 [64, 64, 512], P('pix', None, ('groups', 'dp')), parts along dimension 2
- grad_weights: float32 [8, 64, 64], P('groups'), parts along dimension 0
- grad_bias: float32 [128], P('groups'), parts along dimension 0
The draws below stay inside these ranges and needn't reach their ends.
There are 2 independent parts, one for each index of `groups`. The reference program is written for one: setup_inputs(seed, part) draws one part's arguments, and reference() takes and returns one part's arrays. A program takes and returns all parts, laid end to end along the dimension named above; an argument that names none is the same for every part. Nothing has to cross between parts.
Inputs may be any that keep to these rules, and one draw needn't show every extreme that they name: `send_blocks`: for device p and direction d (to devices p + 1, p - 1, p + 2, p - 2 modulo 8, in this order), 2 distinct local block numbers of device p; no block is listed in two directions. `neighbours`: column 0 names a local block or a received slot 8 + d * 2 + s; every received slot is named by exactly one row, every local block by column 0 of at most one row. Column 1 names a local block other than the row's own, every local block by exactly one row. Both neighbour relations are symmetric. `lap_tiles`: the operator is symmetric: the tile of block b in the row of block a is the transpose of the tile of block a in the row of block b, and a block's own tile is symmetric.
All inputs are finite; a program needn't handle non-finite values. No bound on the sum of `pixel_mask` on one device may be relied on, other than what follows from the above.
Results may differ from the reference program's by a relative error of at most 0.0047.
Values may be sent and summed in bfloat16 or wider, within the bound.
No kernel may reach another device: no remote copies, remote signals or barrier semaphores. Data moves between devices by JAX's collectives and lax.ppermute only.
A program may use at most 64 MiB of HBM per device.

```python
import math
import jax
import jax.numpy as jnp
from jax import lax

CIN = 64
COUT = 64
ORDER = 4
BP = 64
NBR = 9
SLOT = 2
BLK_DEV = 8
BLOCKS = 64
MAPS = 4
N_PIX = 8


DIRECTIONS = (1, -1, 2, -2)


def block_roles(base_key, tag_value):
    order_key = jax.random.fold_in(base_key, tag_value)
    device_keys = jax.random.split(order_key, N_PIX)

    def one_device(sub_key):
        return jax.random.permutation(sub_key, BLK_DEV)
    block_order = jax.vmap(one_device)(device_keys).astype(jnp.int32)
    role_of = jnp.argsort(block_order, axis=1).astype(jnp.int32)
    return (block_order, role_of)


def draw_send_blocks(key, part):
    block_order, role_of = block_roles(key, 11)
    return block_order[:, :4 * SLOT].reshape(N_PIX, 4, SLOT)


def draw_neighbours(key, part):
    block_order, role_of = block_roles(key, 11)
    second_order, second_role = block_roles(key, 12)
    is_cross = role_of < 4 * SLOT
    heading = jnp.minimum(role_of // SLOT, 3)
    slot_index = role_of % SLOT
    halo_ids = BLK_DEV + jnp.bitwise_xor(heading, 1) * SLOT + slot_index
    pair_role = jnp.where(is_cross, role_of, jnp.bitwise_xor(role_of, 1))
    partner = jnp.take_along_axis(block_order, pair_role, axis=1)
    extra_ids = jnp.where(is_cross, halo_ids, partner)
    second_partner = jnp.take_along_axis(second_order, jnp.bitwise_xor(second_role, 1), axis=1)
    columns = jnp.stack([extra_ids, second_partner], axis=2)
    return columns.reshape(N_PIX * BLK_DEV, 2).astype(jnp.int32)


def transpose_tiles(tiles_in):
    return jnp.swapaxes(tiles_in, -1, -2)


def draw_lap_tiles(key, part):
    block_order, role_of = block_roles(key, 11)
    second_order, second_role = block_roles(key, 12)
    tile_shape = (N_PIX, BLK_DEV, BP, BP)
    spread_scale = 0.25 * 0.6666667 / math.sqrt(BP)

    def fresh_tiles(tag_value):
        sub_key = jax.random.fold_in(key, tag_value)
        return jax.random.normal(sub_key, tile_shape, jnp.float32) * spread_scale
    raw_self = fresh_tiles(31)
    self_tile = (raw_self + transpose_tiles(raw_self)) * 0.70710678
    cycle_tiles = [self_tile]
    for reach in (1, 2, 3):
        ahead_tile = fresh_tiles(40 + reach)
        behind = transpose_tiles(jnp.roll(ahead_tile, reach, axis=1))
        cycle_tiles.append(behind)
        cycle_tiles.append(ahead_tile)
    cross_draw = fresh_tiles(33)
    pair_draw = fresh_tiles(34)
    second_draw = fresh_tiles(35)
    device = jnp.arange(N_PIX, dtype=jnp.int32)[:, None]
    heading = jnp.minimum(role_of // SLOT, 3)
    slot_index = role_of % SLOT
    positive = heading % 2 == 0
    travel = jnp.array(DIRECTIONS, dtype=jnp.int32)[heading]
    owner_device = jnp.where(positive, device, (device + travel) % N_PIX)
    edge_index = heading // 2 * SLOT + slot_index
    cross_tile = cross_draw[owner_device, edge_index]
    cross_tile = jnp.where(positive[..., None, None], cross_tile, transpose_tiles(cross_tile))
    local_index = jnp.maximum(role_of - 4 * SLOT, 0)
    pair_tile = pair_draw[device, local_index // 2]
    pair_tile = jnp.where((local_index % 2 == 0)[..., None, None], pair_tile, transpose_tiles(pair_tile))
    extra_tile = jnp.where((role_of < 4 * SLOT)[..., None, None], cross_tile, pair_tile)
    second_tile = second_draw[device, second_role // 2]
    second_tile = jnp.where((second_role % 2 == 0)[..., None, None], second_tile, transpose_tiles(second_tile))
    stacked = jnp.stack(cycle_tiles + [extra_tile, second_tile], axis=3)
    return stacked.reshape(N_PIX * BLK_DEV, BP, 9 * BP).astype(jnp.bfloat16)


def place_ends(entries, stream_key, low, top_value):
    index_at = [jax.random.randint(jax.random.fold_in(stream_key, axis), (), 0, length) for axis, length in enumerate(entries.shape)]
    longest = entries.shape.index(max(entries.shape))
    neighbour = index_at[:longest] + [(index_at[longest] + 1) % entries.shape[longest]] + index_at[longest + 1:]
    return entries.at[tuple(index_at)].set(low).at[tuple(neighbour)].set(top_value)


def level_of(own_key, dims, cuts, smallest, top_value):
    def one(dim, shards_of):
        heights = jax.random.uniform(jax.random.fold_in(jax.random.fold_in(own_key, 6), dim), (shards_of,), jnp.float32, smallest / len(cuts), top_value / len(cuts))
        return jnp.repeat(jnp.exp(heights), dims[dim] // shards_of).reshape((-1,) + (1,) * (len(dims) - dim - 1))

    loudness = one(*cuts[0])
    for cut in cuts[1:]:
        loudness = loudness * one(*cut)
    return loudness


def noise(key, extent, scale, limit, cuts=(), held_as=jnp.bfloat16):
    values = scale * jax.random.normal(key, extent, jnp.float32)
    if cuts:
        values = values * level_of(key, extent, cuts, -0.22, 0.18)
    return jnp.clip(values, -limit, limit).astype(held_as)


def setup_inputs(seed: int = 0, part: int = 0) -> dict:
    keys = jax.random.split(jax.random.key(seed), 9)
    part_keys = jax.random.split(jax.random.fold_in(keys[8], part), 9)
    features = noise(part_keys[0], (BLOCKS, BP, MAPS * CIN), 1.0, 6.0, ((0, 8), (2, 2)))
    cheb_weights = noise(keys[1], (ORDER, CIN, COUT), (ORDER * CIN) ** -0.5, 0.375)
    out_bias = noise(keys[2], (COUT,), 0.5, 3.0, (), jnp.float32)
    lap_tiles = draw_lap_tiles(jax.random.fold_in(keys[8], 71), part)
    neighbours = draw_neighbours(jax.random.fold_in(keys[8], 71), part)
    send_blocks = draw_send_blocks(jax.random.fold_in(keys[8], 71), part)
    pixel_mask = place_ends((jax.random.randint(keys[6], (BLOCKS, BP), 0, 4) < 3).astype(jnp.int32), jax.random.fold_in(keys[6], 1), 0, 1)
    cotangent = noise(part_keys[7], (BLOCKS, BP, MAPS * COUT), 1.0, 6.0, ((0, 8), (2, 2)))
    return dict(features=features, cheb_weights=cheb_weights, out_bias=out_bias, lap_tiles=lap_tiles, neighbours=neighbours, send_blocks=send_blocks, pixel_mask=pixel_mask, cotangent=cotangent)


DIRECTIONS = (1, -1, 2, -2)
CYCLE_STEPS = (0, -1, 1, -2, 2, -3, 3)

def global_rows(neighbours, send_blocks):
    extra_rows = neighbours.reshape(N_PIX, BLK_DEV, 2).astype(jnp.int32)
    local_ids = jnp.arange(BLK_DEV, dtype=jnp.int32)
    cycle_rows = jnp.stack([(local_ids + offset) % BLK_DEV for offset in CYCLE_STEPS], axis=1)
    cycle_rows = jnp.broadcast_to(cycle_rows[None, :, :], (N_PIX, BLK_DEV, len(CYCLE_STEPS))).astype(jnp.int32)
    local_rows = jnp.concatenate([cycle_rows, extra_rows], axis=2)
    device = jnp.arange(N_PIX, dtype=jnp.int32)[:, None, None]
    beyond = jnp.maximum(local_rows - BLK_DEV, 0)
    heading = jnp.minimum(beyond // SLOT, 3)
    slot_index = beyond % SLOT
    travel = jnp.array(DIRECTIONS, dtype=jnp.int32)[heading]
    source = (device - travel) % N_PIX
    remote = source * BLK_DEV + send_blocks[source, heading, slot_index].astype(jnp.int32)
    own_rows = device * BLK_DEV + local_rows
    return jnp.where(local_rows < BLK_DEV, own_rows, remote).reshape(BLOCKS, NBR)

def forward_apply(values, lap_tiles, global_ids, keep_mask):
    masked_values = values * keep_mask
    running = jnp.zeros(values.shape, jnp.float32)
    for column in range(NBR):
        tile_block = lap_tiles[:, :, column * BP:(column + 1) * BP].astype(jnp.float32)
        picked = masked_values[global_ids[:, column]].astype(jnp.float32)
        running = running + jnp.einsum('bpq,bql->bpl', tile_block, picked)
    return running * keep_mask

def adjoint_apply(values, lap_tiles, global_ids, keep_mask):
    spread = (values * keep_mask).astype(jnp.float32)
    running = jnp.zeros(values.shape, jnp.float32)
    for column in range(NBR):
        tile_block = lap_tiles[:, :, column * BP:(column + 1) * BP].astype(jnp.float32)
        partial_terms = jnp.einsum('bpq,bpl->bql', tile_block, spread)
        running = running.at[global_ids[:, column]].add(partial_terms)
    return running * keep_mask

def reference(features, cheb_weights, out_bias, lap_tiles, neighbours, send_blocks, pixel_mask, cotangent):
    global_ids = global_rows(neighbours, send_blocks)
    keep_mask = pixel_mask.astype(jnp.bfloat16)[:, :, None]
    cheb_terms = [features]
    for degree in range(1, ORDER):
        applied = forward_apply(cheb_terms[-1], lap_tiles, global_ids, keep_mask)
        if degree == 1:
            cheb_terms.append(applied.astype(jnp.bfloat16))
        else:
            cheb_terms.append((2.0 * applied - cheb_terms[-2].astype(jnp.float32)).astype(jnp.bfloat16))
    weights_wide = cheb_weights.astype(jnp.float32)
    flat_rows = BLOCKS * BP
    mixed_sum = jnp.zeros((flat_rows, MAPS, COUT), jnp.float32)
    for degree in range(ORDER):
        term_block = cheb_terms[degree].reshape(flat_rows, MAPS, CIN).astype(jnp.float32)
        mixed_sum = mixed_sum + jnp.einsum('rmc,co->rmo', term_block, weights_wide[degree])
    output_maps = (mixed_sum + out_bias.astype(jnp.float32)).reshape(BLOCKS, BP, MAPS * COUT).astype(jnp.bfloat16)
    upstream = cotangent.reshape(flat_rows, MAPS, COUT).astype(jnp.float32)

    def direct(degree):
        return jnp.einsum('rmo,co->rmc', upstream, weights_wide[degree]).reshape(BLOCKS, BP, MAPS * CIN)
    adjoints = [None] * ORDER
    for degree in range(ORDER - 1, 0, -1):
        running = direct(degree)
        if degree + 1 < ORDER:
            running = running + 2.0 * adjoint_apply(adjoints[degree + 1], lap_tiles, global_ids, keep_mask)
        if degree + 2 < ORDER:
            running = running - adjoints[degree + 2].astype(jnp.float32)
        adjoints[degree] = running.astype(jnp.bfloat16)
    running = direct(0) + adjoint_apply(adjoints[1], lap_tiles, global_ids, keep_mask)
    running = running - adjoints[2].astype(jnp.float32)
    grad_features = running.astype(jnp.bfloat16)
    factor = 1.0 / math.sqrt(BLOCKS * BP * MAPS)
    grad_list = []
    for degree in range(ORDER):
        term_block = cheb_terms[degree].reshape(flat_rows, MAPS, CIN).astype(jnp.float32)
        grad_list.append(jnp.einsum('rmc,rmo->co', term_block, upstream))
    grad_weights = jnp.stack(grad_list) * factor
    grad_bias = lax.optimization_barrier(jnp.sum(upstream, axis=(0, 1))) * factor
    return (output_maps, grad_features, grad_weights, grad_bias)
```

```python
import functools
import math

import jax
import jax.numpy as jnp
from jax import lax
from jax.experimental import pallas as pl
from jax.experimental.pallas import tpu as pltpu
from jax.sharding import PartitionSpec as P

CYCLE_STEPS = (0, -1, 1, -2, 2, -3, 3)
ROW_SPLIT = 2
F32 = jnp.float32
BF16 = jnp.bfloat16


def pair_of(index, pairing, count):
    if pairing == 0:
        return index ^ 1
    if pairing == 1:
        return (index + 1 if index % 2 else index - 1) % count
    low = index % 4 < 2
    step = 2 if low == (pairing == 2) else -2
    return (index + step) % count


def exchange(block, pairing):
    count = lax.axis_size("pix")
    route = [(pair_of(i, pairing, count), i) for i in range(count)]
    return lax.ppermute(block, "pix", route)


def send_heading(pairing, device):
    if pairing < 2:
        return (device + pairing) % 2
    return 2 + (device // 2 + pairing) % 2


def matmul(left, right):
    return jnp.dot(left, right, preferred_element_type=F32)


def matmul_tn(left, right):
    return lax.dot_general(left, right, (((0,), (0,)), ((), ())), preferred_element_type=F32)


def matmul_nt(left, right):
    return lax.dot_general(left, right, (((1,), (1,)), ((), ())), preferred_element_type=F32)


def pack_kernel(
    rows_ref, lists_ref, mask_ref, feat_ref, cot_ref, lap_ref,
    send0, send1, send2, send3, ring_ref, near_ref, far_ref, part_ref,
    value, paired, keep, keep_row,
):
    blocks, pixels, lanes = feat_ref.shape
    group = blocks // ROW_SPLIT
    device = lax.axis_index("pix")
    keep[...] = mask_ref[...].astype(F32)
    for b in range(blocks):
        keep_row[:, b * pixels:(b + 1) * pixels] = jnp.broadcast_to(keep[b:b + 1, :], (8, pixels))
        value[b, :, :lanes] = feat_ref[b]
        value[b, :, lanes:] = cot_ref[b]
    diagonal = lax.broadcasted_iota(jnp.int32, (pixels, pixels), 0) == lax.broadcasted_iota(
        jnp.int32, (pixels, pixels), 1
    )
    ring_ref[...] = jnp.zeros_like(ring_ref)
    near_ref[...] = jnp.zeros_like(near_ref)
    far_ref[...] = jnp.zeros_like(far_ref)
    cycle = len(CYCLE_STEPS) * pixels
    for a in range(blocks):
        column = jnp.sum(
            jnp.where(diagonal, keep[a:a + 1, :], 0.0), axis=1, keepdims=True
        )
        rows = slice(a * pixels, (a + 1) * pixels)
        for j, step in enumerate(CYCLE_STEPS):
            b = (a + step) % blocks
            tile = lap_ref[a, :, j * pixels:(j + 1) * pixels].astype(F32)
            both = column * keep[b:b + 1, :]
            ring_ref[rows, b * pixels:(b + 1) * pixels] = (tile * both).astype(BF16)
        g, t = a // group, a % group
        spot = slice(t * pixels, (t + 1) * pixels)
        second = rows_ref[a, 1]
        tile = lap_ref[a, :, cycle + pixels:cycle + 2 * pixels].astype(F32)
        near_ref[g, spot, spot] = (tile * (column * keep[pl.ds(second, 1), :])).astype(BF16)
        tile = lap_ref[a, :, cycle:cycle + pixels].astype(F32)
        far_ref[g, spot, spot] = (tile * column).astype(BF16)
        paired[a] = value[second]
    whole = value[...].reshape(blocks * pixels, 2 * lanes)
    part = matmul(ring_ref[...], whole)
    for g in range(ROW_SPLIT):
        mates = paired[g * group:(g + 1) * group].reshape(group * pixels, 2 * lanes)
        rows = slice(g * group * pixels, (g + 1) * group * pixels)
        total = part[rows] + matmul(near_ref[g], mates)
        part_ref[g * group:(g + 1) * group] = total.reshape(group, pixels, 2 * lanes)
    for pairing, send in enumerate((send0, send1, send2, send3)):
        heading = send_heading(pairing, device)
        slots = lists_ref.shape[2]
        for s in range(slots):
            b = lists_ref[0, heading, s]
            base = s * 2 * pixels
            send[base:base + pixels, :] = value[b]
            send[base + pixels:base + 2 * pixels, :] = part_ref[b].astype(BF16)
        tail = slots * 2 * pixels
        send[tail:, :] = jnp.zeros((16, 2 * lanes), BF16)
        first = keep[pl.ds(lists_ref[0, heading, 0], 1), :]
        last = keep[pl.ds(lists_ref[0, heading, 1], 1), :]
        which = lax.broadcasted_iota(jnp.int32, (16, pixels), 0)
        send[tail:, :pixels] = jnp.where(
            which == 0, first, jnp.where(which == 1, last, 0.0)
        ).astype(BF16)


def row_of_slot(rows_ref, slot):
    blocks = rows_ref.shape[0]
    found = jnp.int32(0)
    for a in range(blocks):
        found = jnp.where(rows_ref[a, 0] == blocks + slot, a, found)
    return found


def middle_kernel(
    rows_ref, lists_ref, feat_ref, cot_ref, ring_ref, near_ref, far_ref, part_ref,
    got0, got1, got2, got3,
    one_ref, two_ref, cross_ref, send0, send1, send2, send3, sums_ref,
    value, halo, halo_part, paired, keep_far, scratch_two,
):
    blocks, pixels, lanes = feat_ref.shape
    group = blocks // ROW_SPLIT
    flat = blocks * pixels
    device = lax.axis_index("pix")
    for b in range(blocks):
        value[b, :, :lanes] = feat_ref[b]
        value[b, :, lanes:] = cot_ref[b]
    slots = lists_ref.shape[2]
    tail = slots * 2 * pixels
    for pairing, got in enumerate((got0, got1, got2, got3)):
        heading = send_heading(pairing, device) ^ 1
        flags = got[tail:, :pixels].astype(F32)
        for s in range(slots):
            row = row_of_slot(rows_ref, heading * slots + s)
            base = s * 2 * pixels
            halo[row] = got[base:base + pixels, :]
            halo_part[row] = got[base + pixels:base + 2 * pixels, :]
            keep_far[pl.ds(row, 1), :] = flags[s:s + 1, :]
    cross_ref[...] = jnp.zeros_like(cross_ref)
    for a in range(blocks):
        g, t = a // group, a % group
        spot = slice(t * pixels, (t + 1) * pixels)
        tile = far_ref[g, spot, spot].astype(F32)
        cross_ref[g, spot, spot] = (tile * keep_far[a:a + 1, :]).astype(BF16)
    width = 2 * lanes
    size = group * pixels
    for g in range(ROW_SPLIT):
        mine = slice(g * group, (g + 1) * group)
        other = halo[mine].reshape(size, width)
        total = part_ref[mine].reshape(size, width) + matmul(cross_ref[g], other)
        one_ref[mine] = total.astype(BF16).reshape(group, pixels, width)
        own = value[mine].reshape(size, width)
        total = halo_part[mine].reshape(size, width).astype(F32) + matmul_tn(cross_ref[g], own)
        halo[mine] = total.astype(BF16).reshape(group, pixels, width)
    for a in range(blocks):
        paired[a] = one_ref[rows_ref[a, 1]]
    applied = matmul(ring_ref[...], one_ref[...].reshape(flat, width))
    for g in range(ROW_SPLIT):
        mine = slice(g * group, (g + 1) * group)
        total = applied[g * size:(g + 1) * size]
        total = total + matmul(near_ref[g], paired[mine].reshape(size, width))
        total = total + matmul(cross_ref[g], halo[mine].reshape(size, width))
        total = 2.0 * total - value[mine].reshape(size, width).astype(F32)
        total = total.astype(BF16).reshape(group, pixels, width)
        two_ref[mine] = total
    for pairing, send in enumerate((send0, send1, send2, send3)):
        heading = send_heading(pairing, device)
        for s in range(slots):
            send[s * pixels:(s + 1) * pixels, :] = two_ref[lists_ref[0, heading, s]]
    zero = value[...].reshape(flat, width)
    one = one_ref[...].reshape(flat, width)
    two = two_ref[...].reshape(flat, width)
    half = lanes // 2
    cot = zero[:, lanes:]
    cot_one = one[:, lanes:]
    low = matmul_tn(jnp.concatenate([zero[:, :lanes], one[:, :lanes]], axis=1), cot)
    high = matmul_tn(jnp.concatenate([one[:, :lanes], two[:, :lanes]], axis=1), cot_one)

    def trace(product, start):
        return (
            product[start:start + half, :half] + product[start + half:start + lanes, half:]
        )

    zeroth = trace(low, 0)
    first = trace(low, lanes)
    second = 2.0 * trace(high, 0) - zeroth
    third = 2.0 * trace(high, lanes) - first
    sums_ref[:half, :half] = zeroth
    sums_ref[:half, half:] = first
    sums_ref[half:lanes, :half] = second
    sums_ref[half:lanes, half:] = third
    sums_ref[lanes:, :] = jnp.broadcast_to(
        jnp.sum(cot.astype(F32), axis=0, keepdims=True), (8, lanes)
    )


def last_kernel(
    rows_ref, feat_ref, cot_ref, weight_ref, bias_ref, ring_ref, near_ref, cross_ref, one_ref,
    two_ref, got0, got1, got2, got3,
    out_ref, grad_ref,
    halo, paired, mix, mix_wide,
):
    blocks, pixels, lanes = feat_ref.shape
    terms, half, _ = weight_ref.shape
    group = blocks // ROW_SPLIT
    flat, width, size = blocks * pixels, 2 * lanes, group * pixels
    device = lax.axis_index("pix")
    slots = got0.shape[0] // pixels
    for pairing, got in enumerate((got0, got1, got2, got3)):
        heading = send_heading(pairing, device) ^ 1
        for s in range(slots):
            row = row_of_slot(rows_ref, heading * slots + s)
            halo[row] = got[s * pixels:(s + 1) * pixels, :]
    for a in range(blocks):
        paired[a] = two_ref[rows_ref[a, 1]]
    mix[...] = jnp.zeros_like(mix)
    mix_wide[...] = jnp.zeros_like(mix_wide)
    for k in range(terms):
        for m in range(lanes // half):
            spot = slice(m * half, (m + 1) * half)
            shifted = slice(k * lanes + m * half, k * lanes + (m + 1) * half)
            mix[shifted, spot] = weight_ref[k]
            mix_wide[spot, shifted] = weight_ref[k]
    applied = matmul(ring_ref[...], two_ref[...].reshape(flat, width))
    bias = jnp.concatenate([bias_ref[...]] * (lanes // half), axis=1)
    for g in range(ROW_SPLIT):
        mine = slice(g * group, (g + 1) * group)
        total = applied[g * size:(g + 1) * size]
        total = total + matmul(near_ref[g], paired[mine].reshape(size, width))
        total = total + matmul(cross_ref[g], halo[mine].reshape(size, width))
        one = one_ref[mine].reshape(size, width)
        two = two_ref[mine].reshape(size, width)
        three = (2.0 * total - one.astype(F32)).astype(BF16)
        feat = feat_ref[mine].reshape(size, lanes)
        cot = cot_ref[mine].reshape(size, lanes)
        forward = jnp.concatenate(
            [feat, one[:, :lanes], two[:, :lanes], three[:, :lanes]], axis=1
        )
        backward = jnp.concatenate(
            [cot, one[:, lanes:], two[:, lanes:], three[:, lanes:]], axis=1
        )
        out = matmul(forward, mix[...]) + bias
        out_ref[mine] = out.astype(BF16).reshape(group, pixels, lanes)
        grad = matmul_nt(backward, mix_wide[...])
        grad_ref[mine] = grad.astype(BF16).reshape(group, pixels, lanes)


def finish_kernel(factor, mine_ref, other_ref, weight_ref, bias_ref):
    total = (mine_ref[...] + other_ref[...]) * factor
    terms, half, _ = weight_ref.shape
    lanes = 2 * half
    for k in range(terms):
        rows, cols = k // 2 * half, k % 2 * half
        weight_ref[k] = total[rows:rows + half, cols:cols + half]
    bias = total[lanes:lanes + 1, :]
    bias_ref[...] = bias[:, :half] + bias[:, half:]


def call(kernel, outs, ins, scratch, flops):
    vmem = pl.BlockSpec(memory_space=pltpu.VMEM)
    smem = pl.BlockSpec(memory_space=pltpu.SMEM)
    touched = sum(math.prod(x.shape) * x.dtype.itemsize for x in [*ins, *outs])
    return pl.pallas_call(
        kernel,
        out_shape=outs,
        in_specs=[smem if i < 2 and x.dtype == jnp.int32 else vmem for i, x in enumerate(ins)],
        out_specs=[vmem] * len(outs),
        scratch_shapes=scratch,
        cost_estimate=pl.CostEstimate(flops=flops, transcendentals=0, bytes_accessed=touched),
        compiler_params=pltpu.CompilerParams(vmem_limit_bytes=32 << 20),
    )(*ins)


def local(
    features, cheb_weights, out_bias, lap_tiles, neighbours, send_blocks, pixel_mask, cotangent
):
    blocks, pixels, lanes = features.shape
    terms, chan_in, chan_out = cheb_weights.shape
    slots = send_blocks.shape[2]
    width, flat = 2 * lanes, blocks * pixels
    size = flat // ROW_SPLIT
    shape = jax.ShapeDtypeStruct
    apply_flops = 2 * flat * width * (flat + 2 * size)

    operator = [
        shape((flat, flat), BF16),
        shape((ROW_SPLIT, size, size), BF16),
        shape((ROW_SPLIT, size, size), BF16),
    ]
    field = shape((blocks, pixels, width), BF16)
    wide = shape((blocks, pixels, width), F32)
    *sends, ring, near, far, part = call(
        pack_kernel,
        [shape((slots * 2 * pixels + 16, width), BF16)] * 4 + operator + [wide],
        [neighbours, send_blocks, pixel_mask, features, cotangent, lap_tiles],
        [
            pltpu.VMEM((blocks, pixels, width), BF16),
            pltpu.VMEM((blocks, pixels, width), BF16),
            pltpu.VMEM((blocks, pixels), F32),
            pltpu.VMEM((8, flat), F32),
        ],
        apply_flops,
    )
    order = (1, 0, 2, 3)
    got = {k: exchange(sends[k], k) for k in order}
    one, two, cross, *rest = call(
        middle_kernel,
        [field, field, operator[1]]
        + [shape((slots * pixels, width), BF16)] * 4
        + [shape((lanes + 8, lanes), F32)],
        [neighbours, send_blocks, features, cotangent, ring, near, far, part]
        + [got[k] for k in range(4)],
        [
            pltpu.VMEM((blocks, pixels, width), BF16),
            pltpu.VMEM((blocks, pixels, width), BF16),
            pltpu.VMEM((blocks, pixels, width), BF16),
            pltpu.VMEM((blocks, pixels, width), BF16),
            pltpu.VMEM((blocks, pixels), F32),
            pltpu.VMEM((8, 128), F32),
        ],
        2 * apply_flops,
    )
    sends, sums = rest[:4], rest[4]
    got = {k: exchange(sends[k], k) for k in order}
    output_maps, grad_features = call(
        last_kernel,
        [shape(features.shape, BF16), shape(features.shape, BF16)],
        [neighbours, features, cotangent, cheb_weights, out_bias.reshape(1, chan_out)]
        + [ring, near, cross, one, two]
        + [got[k] for k in range(4)],
        [
            pltpu.VMEM((blocks, pixels, width), BF16),
            pltpu.VMEM((blocks, pixels, width), BF16),
            pltpu.VMEM((terms * lanes, lanes), BF16),
            pltpu.VMEM((lanes, terms * lanes), BF16),
        ],
        2 * apply_flops,
    )
    count = lax.axis_size("pix")
    pair = lax.axis_size("dp")
    factor = 1.0 / math.sqrt(flat * (lanes // chan_in) * count * pair)
    other = lax.ppermute(sums, "dp", [(i ^ 1, i) for i in range(pair)])
    reach = 1
    while reach < count:
        sums = sums + other
        other = lax.ppermute(sums, "pix", [(i ^ reach, i) for i in range(count)])
        reach *= 2
    grad_weights, grad_bias = call(
        functools.partial(finish_kernel, factor),
        [shape(cheb_weights.shape, F32), shape((1, chan_out), F32)],
        [sums, other],
        [],
        sums.size,
    )
    return output_maps, grad_features, grad_weights, grad_bias.reshape(chan_out)


def solution(mesh):
    return jax.shard_map(
        local,
        mesh=mesh,
        in_specs=(
            P("pix", None, ("groups", "dp")),
            P(),
            P(),
            P("pix", None, None),
            P("pix", None),
            P("pix", None, None),
            P("pix", None),
            P("pix", None, ("groups", "dp")),
        ),
        out_specs=(
            P("pix", None, ("groups", "dp")),
            P("pix", None, ("groups", "dp")),
            P("groups", None, None),
            P("groups"),
        ),
        check_vma=False,
    )
```

```python
import functools
import math

import jax
import jax.numpy as jnp
from jax import lax
from jax.experimental import pallas as pl
from jax.experimental.pallas import tpu as pltpu
from jax.sharding import PartitionSpec as P

CYCLE_STEPS = (0, -1, 1, -2, 2, -3, 3)
ORDER = (1, 3, 0, 2)
F32 = jnp.float32
BF16 = jnp.bfloat16


def pair_of(index, pairing, count):
    if pairing == 0:
        return index ^ 1
    if pairing == 1:
        return (index + 1 if index % 2 else index - 1) % count
    low = index % 4 < 2
    step = 2 if low == (pairing == 2) else -2
    return (index + step) % count


def exchange(block, pairing):
    count = lax.axis_size("pix")
    route = [(pair_of(i, pairing, count), i) for i in range(count)]
    return lax.ppermute(block, "pix", route)


def send_heading(pairing, device):
    if pairing < 2:
        return (device + pairing) % 2
    return 2 + (device // 2 + pairing) % 2


def matmul(left, right):
    return jnp.dot(left, right, preferred_element_type=F32)


def matmul_tn(left, right):
    return lax.dot_general(left, right, (((0,), (0,)), ((), ())), preferred_element_type=F32)


def matmul_nt(left, right):
    return lax.dot_general(left, right, (((1,), (1,)), ((), ())), preferred_element_type=F32)


def row_of_slot(rows_ref, slot):
    blocks = rows_ref.shape[1]
    found = jnp.int32(0)
    for a in range(blocks):
        found = jnp.where(rows_ref[0, a] == blocks + slot, a, found)
    return found


def ring_rows(field, a):
    blocks = field.shape[0]
    return [field[(a + step) % blocks] for step in CYCLE_STEPS]


def pack_kernel(
    rows_hbm, lists_hbm, mask_hbm, feat_hbm, cot_hbm, lap_hbm, weight_hbm, bias_hbm,
    *refs,
):
    sends, (value, keep, part, rows_ref, lists_ref, mix, mix_last, bias_row) = refs[:4], refs[4:12]
    mask, lap, weight, bias, sem = refs[12:]
    blocks, pixels, lanes = feat_hbm.shape
    slots = lists_hbm.shape[1]
    cycle = len(CYCLE_STEPS) * pixels
    device = lax.axis_index("pix")
    copies = [
        pltpu.make_async_copy(mask_hbm, mask, sem.at[0]),
        pltpu.make_async_copy(feat_hbm, value.at[:, :, pl.ds(0, lanes)], sem.at[1]),
        pltpu.make_async_copy(cot_hbm, value.at[:, :, pl.ds(lanes, lanes)], sem.at[2]),
        pltpu.make_async_copy(lap_hbm, lap, sem.at[3]),
        pltpu.make_async_copy(rows_hbm, rows_ref, sem.at[4]),
        pltpu.make_async_copy(lists_hbm, lists_ref, sem.at[5]),
        pltpu.make_async_copy(weight_hbm, weight, sem.at[6]),
        pltpu.make_async_copy(bias_hbm, bias, sem.at[7]),
    ]
    for copy in copies:
        copy.start()
    diagonal = lax.broadcasted_iota(jnp.int32, (pixels, pixels), 0) == lax.broadcasted_iota(
        jnp.int32, (pixels, pixels), 1
    )
    copies[0].wait()
    for a in range(blocks):
        row = mask[a:a + 1, :].astype(F32)
        column = jnp.sum(jnp.where(diagonal, row, 0.0), axis=1, keepdims=True)
        keep[a] = jnp.broadcast_to(column, (pixels, 2 * lanes)).astype(BF16)
    copies[1].wait()
    copies[2].wait()
    masked = [value[a] * keep[a] for a in range(blocks)]
    for a in range(blocks):
        value[a] = masked[a]
    copies[4].wait()
    copies[5].wait()
    copies[3].wait()
    for a in range(blocks):
        total = matmul(lap[a, :, :cycle], jnp.concatenate(ring_rows(value, a), axis=0))
        total = total + matmul(lap[a, :, cycle + pixels:], value[rows_ref[1, a]])
        part[a] = total * keep[a].astype(F32)
    tail = slots * 2 * pixels
    which = lax.broadcasted_iota(jnp.int32, (16, pixels), 0)
    for pairing, send in zip(ORDER, sends):
        heading = send_heading(pairing, device)
        flags = jnp.zeros((16, pixels), F32)
        for s in range(slots):
            b = lists_ref[0, s, heading]
            base = s * 2 * pixels
            send[base:base + pixels, :] = value[b]
            send[base + pixels:base + 2 * pixels, :] = part[b].astype(BF16)
            flags = jnp.where(which == s, mask[pl.ds(b, 1), :].astype(F32), flags)
        send[tail:, :] = jnp.zeros((16, 2 * lanes), BF16)
        send[tail:, :pixels] = flags.astype(BF16)
    copies[6].wait()
    copies[7].wait()
    terms, half, _ = weight.shape
    mix[...] = jnp.zeros_like(mix)
    mix_last[...] = jnp.zeros_like(mix_last)
    for m in range(lanes // half):
        spot = slice(m * half, (m + 1) * half)
        for k in range(terms - 1):
            shifted = slice(k * lanes + m * half, k * lanes + (m + 1) * half)
            mix[spot, shifted] = weight[k]
        mix_last[spot, spot] = weight[terms - 1]
        bias_row[:, spot] = bias[...]


def middle_kernel(
    rows_ref, lists_ref, feat_ref, cot_ref, lap, value, keep, part, *refs,
):
    gots, (one, two, spread), sends, (sums,) = refs[:4], refs[4:7], refs[7:11], refs[11:12]
    halo, halo_part, keep_far = refs[12:]
    blocks, pixels, lanes = feat_ref.shape
    slots = lists_ref.shape[1]
    cycle = len(CYCLE_STEPS) * pixels
    flat, width = blocks * pixels, 2 * lanes
    device = lax.axis_index("pix")
    tail = slots * 2 * pixels
    for pairing, got in zip(ORDER, gots):
        heading = send_heading(pairing, device) ^ 1
        flags = got[tail:, :pixels].astype(F32)
        for s in range(slots):
            row = row_of_slot(rows_ref, heading * slots + s)
            base = s * 2 * pixels
            halo[row] = got[base:base + pixels, :]
            halo_part[row] = got[base + pixels:base + 2 * pixels, :]
            keep_far[pl.ds(row, 1), :] = flags[s:s + 1, :]
    for a in range(blocks):
        cross = lap[a, :, cycle:cycle + pixels] * keep_far[a:a + 1, :].astype(BF16)
        total = part[a] + matmul(cross, halo[a]) * keep[a].astype(F32)
        one[a] = total.astype(BF16)
        total = halo_part[a].astype(F32) + matmul_tn(cross, value[a])
        halo[a] = total.astype(BF16)
    for a in range(blocks):
        near = ring_rows(one, a) + [halo[a], one[rows_ref[1, a]]]
        total = matmul(lap[a], jnp.concatenate(near, axis=0)) * keep[a].astype(F32)
        base = jnp.concatenate([feat_ref[a], cot_ref[a]], axis=1).astype(F32)
        fresh = (2.0 * total - base).astype(BF16)
        two[a] = fresh
        spread[a] = fresh * keep[a]
    for pairing, send in zip(ORDER, sends):
        heading = send_heading(pairing, device)
        for s in range(slots):
            send[s * pixels:(s + 1) * pixels, :] = spread[lists_ref[0, s, heading]]
    feat = feat_ref[...].reshape(flat, lanes)
    cot = cot_ref[...].reshape(flat, lanes)
    first = one[...].reshape(flat, width)
    second = two[...].reshape(flat, width)
    half = lanes // 2
    low = matmul_tn(jnp.concatenate([feat, first[:, :lanes]], axis=1), cot)
    high = matmul_tn(
        jnp.concatenate([first[:, :lanes], second[:, :lanes]], axis=1), first[:, lanes:]
    )

    def trace(product, start):
        return (
            product[start:start + half, :half] + product[start + half:start + lanes, half:]
        )

    sum_zero = trace(low, 0)
    sum_one = trace(low, lanes)
    sums[:half, :half] = sum_zero
    sums[:half, half:] = sum_one
    sums[half:lanes, :half] = 2.0 * trace(high, 0) - sum_zero
    sums[half:lanes, half:] = 2.0 * trace(high, lanes) - sum_one
    sums[lanes:, :] = jnp.broadcast_to(
        jnp.sum(cot.astype(F32), axis=0, keepdims=True), (8, lanes)
    )


def partial_kernel(feat_ref, cot_ref, mix, bias_row, one, two, out_part, grad_part):
    blocks, pixels, lanes = feat_ref.shape
    flat = blocks * pixels
    first = one[...].reshape(flat, 2 * lanes)
    second = two[...].reshape(flat, 2 * lanes)
    total = jnp.broadcast_to(bias_row[...], (flat, lanes))
    fields = [feat_ref[...].reshape(flat, lanes), first[:, :lanes], second[:, :lanes]]
    for k, field in enumerate(fields):
        total = total + matmul(field, mix[:, k * lanes:(k + 1) * lanes])
    out_part[...] = total.reshape(blocks, pixels, lanes)
    fields = [cot_ref[...].reshape(flat, lanes), first[:, lanes:], second[:, lanes:]]
    total = matmul_nt(jnp.concatenate(fields, axis=1), mix[...])
    grad_part[...] = total.reshape(blocks, pixels, lanes)


def last_kernel(
    rows_ref, lap, keep, one, spread, out_part, grad_part, mix_last, *refs,
):
    gots, (out_ref, grad_ref), (halo, three) = refs[:4], refs[4:6], refs[6:]
    blocks, pixels, lanes = out_part.shape
    device = lax.axis_index("pix")
    slots = gots[0].shape[0] // pixels
    for pairing, got in zip(ORDER, gots):
        heading = send_heading(pairing, device) ^ 1
        for s in range(slots):
            row = row_of_slot(rows_ref, heading * slots + s)
            halo[row] = got[s * pixels:(s + 1) * pixels, :]
    for a in range(blocks):
        near = ring_rows(spread, a) + [halo[a], spread[rows_ref[1, a]]]
        total = matmul(lap[a], jnp.concatenate(near, axis=0)) * keep[a].astype(F32)
        three[a] = (2.0 * total - one[a].astype(F32)).astype(BF16)
    flat = blocks * pixels
    last = three[...].reshape(flat, 2 * lanes)
    total = out_part[...].reshape(flat, lanes) + matmul(last[:, :lanes], mix_last[...])
    out_ref[...] = total.astype(BF16).reshape(blocks, pixels, lanes)
    total = grad_part[...].reshape(flat, lanes) + matmul_nt(last[:, lanes:], mix_last[...])
    grad_ref[...] = total.astype(BF16).reshape(blocks, pixels, lanes)


def finish_kernel(factor, mine, other, weight_ref, bias_ref):
    sums = (mine[...] + other[...]) * factor
    terms, half, _ = weight_ref.shape
    lanes = 2 * half
    for k in range(terms):
        rows, cols = k // 2 * half, k % 2 * half
        weight_ref[k] = sums[rows:rows + half, cols:cols + half]
    bias = sums[lanes:lanes + 1, :]
    bias_ref[...] = bias[:, :half] + bias[:, half:]


def call(kernel, outs, ins, scratch, flops, in_hbm=False):
    vmem = pl.BlockSpec(memory_space=pltpu.VMEM)
    smem = pl.BlockSpec(memory_space=pltpu.SMEM)
    hbm = pl.BlockSpec(memory_space=pltpu.MemorySpace.HBM)
    touched = sum(math.prod(x.shape) * x.dtype.itemsize for x in [*ins, *outs])
    if in_hbm:
        ins = [pltpu.with_memory_space_constraint(x, pltpu.MemorySpace.HBM) for x in ins]

    def place(i, x):
        if in_hbm:
            return hbm
        return smem if i < 2 and x.dtype == jnp.int32 else vmem

    return pl.pallas_call(
        kernel,
        out_shape=outs,
        in_specs=[place(i, x) for i, x in enumerate(ins)],
        out_specs=[smem if x.dtype == jnp.int32 else vmem for x in outs],
        scratch_shapes=scratch,
        cost_estimate=pl.CostEstimate(flops=flops, transcendentals=0, bytes_accessed=touched),
        compiler_params=pltpu.CompilerParams(vmem_limit_bytes=32 << 20),
    )(*ins)


def local(
    features, cheb_weights, out_bias, lap_tiles, neighbours, send_blocks, pixel_mask, cotangent
):
    blocks, pixels, lanes = features.shape
    terms, chan_in, chan_out = cheb_weights.shape
    slots = send_blocks.shape[2]
    width, flat = 2 * lanes, blocks * pixels
    shape = jax.ShapeDtypeStruct
    apply_flops = 2 * flat * width * lap_tiles.shape[2]
    rows = neighbours.T
    lists = send_blocks.transpose(0, 2, 1)

    field = shape((blocks, pixels, width), BF16)
    wide = shape((blocks, pixels, width), F32)
    scratch_field = pltpu.VMEM((blocks, pixels, width), BF16)
    *sends, value, keep, part, rows, lists, mix, mix_last, bias_row = call(
        pack_kernel,
        [shape((slots * 2 * pixels + 16, width), BF16)] * 4 + [field, field, wide]
        + [shape(rows.shape, jnp.int32), shape(lists.shape, jnp.int32)]
        + [shape((lanes, (terms - 1) * lanes), BF16), shape((lanes, lanes), BF16)]
        + [shape((1, lanes), F32)],
        [rows, lists, pixel_mask, features, cotangent, lap_tiles, cheb_weights]
        + [out_bias.reshape(1, chan_out)],
        [
            pltpu.VMEM((blocks, pixels), jnp.int32),
            pltpu.VMEM(lap_tiles.shape, BF16),
            pltpu.VMEM(cheb_weights.shape, BF16),
            pltpu.VMEM((1, chan_out), F32),
            pltpu.SemaphoreType.DMA((8,)),
        ],
        apply_flops,
        in_hbm=True,
    )
    gots = [exchange(send, k) for k, send in zip(ORDER, sends)]
    one, two, spread, *sends, sums = call(
        middle_kernel,
        [field, field, field]
        + [shape((slots * pixels, width), BF16)] * 4
        + [shape((lanes + 8, lanes), F32)],
        [rows, lists, features, cotangent, lap_tiles, value, keep, part, *gots],
        [scratch_field, scratch_field, pltpu.VMEM((blocks, pixels), F32)],
        2 * apply_flops,
    )
    gots = [exchange(send, k) for k, send in zip(ORDER, sends)]
    half_field = shape((blocks, pixels, lanes), F32)
    parts = call(
        partial_kernel,
        [half_field, half_field],
        [features, cotangent, mix, bias_row, one, two],
        [],
        4 * flat * lanes * lanes * (terms - 1),
    )
    count = lax.axis_size("pix")
    pair = lax.axis_size("dp")
    factor = 1.0 / math.sqrt(flat * (lanes // chan_in) * count * pair)
    other = lax.ppermute(sums, "dp", [(i ^ 1, i) for i in range(pair)])
    reach = 1
    while reach < count:
        sums = sums + other
        other = lax.ppermute(sums, "pix", [(i ^ reach, i) for i in range(count)])
        reach *= 2
    output_maps, grad_features = call(
        last_kernel,
        [shape(features.shape, BF16), shape(features.shape, BF16)],
        [rows, lap_tiles, keep, one, spread, *parts, mix_last, *gots],
        [scratch_field, scratch_field],
        2 * apply_flops,
    )
    grad_weights, grad_bias = call(
        functools.partial(finish_kernel, factor),
        [shape(cheb_weights.shape, F32), shape((1, chan_out), F32)],
        [sums, other],
        [],
        sums.size,
    )
    return output_maps, grad_features, grad_weights, grad_bias.reshape(chan_out)


def solution(mesh):
    return jax.shard_map(
        local,
        mesh=mesh,
        in_specs=(
            P("pix", None, ("groups", "dp")),
            P(),
            P(),
            P("pix", None, None),
            P("pix", None),
            P("pix", None, None),
            P("pix", None),
            P("pix", None, ("groups", "dp")),
        ),
        out_specs=(
            P("pix", None, ("groups", "dp")),
            P("pix", None, ("groups", "dp")),
            P("groups", None, None),
            P("groups"),
        ),
        check_vma=False,
    )
```

```python
import functools
import math

import jax
import jax.numpy as jnp
from jax import lax
from jax.experimental import pallas as pl
from jax.experimental.pallas import tpu as pltpu
from jax.sharding import PartitionSpec as P

CYCLE_STEPS = (0, -1, 1, -2, 2, -3, 3)
ORDER = (3, 1, 2, 0)
ORDER_TWO = (0, 1, 3, 2)
TIES = {}
STEPS = (0, 2, 4)
F32 = jnp.float32
BF16 = jnp.bfloat16


def pair_of(index, pairing, count):
    if pairing == 0:
        return index ^ 1
    if pairing == 1:
        return (index + 1 if index % 2 else index - 1) % count
    low = index % 4 < 2
    step = 2 if low == (pairing == 2) else -2
    return (index + step) % count


def exchange(block, pairing):
    count = lax.axis_size("pix")
    route = [(pair_of(i, pairing, count), i) for i in range(count)]
    return lax.ppermute(block, "pix", route)


def send_heading(pairing, device):
    if pairing < 2:
        return (device + pairing) % 2
    return 2 + (device // 2 + pairing) % 2


def matmul(left, right):
    return jnp.dot(left, right, preferred_element_type=F32)


def matmul_tn(left, right):
    return lax.dot_general(left, right, (((0,), (0,)), ((), ())), preferred_element_type=F32)


def matmul_nt(left, right):
    return lax.dot_general(left, right, (((1,), (1,)), ((), ())), preferred_element_type=F32)


def row_of_slot(rows_ref, slot):
    blocks = rows_ref.shape[1]
    found = jnp.int32(0)
    for a in range(blocks):
        found = jnp.where(rows_ref[0, a] == blocks + slot, a, found)
    return found


def ring_rows(field, a):
    blocks = field.shape[0]
    return [field[(a + step) % blocks] for step in CYCLE_STEPS]


def pack_kernel(
    rows_hbm, lists_hbm, mask_hbm, feat_hbm, cot_hbm, lap_hbm,
    *refs,
):
    sends, (value, keep, part, rows_ref, lists_ref) = refs[:4], refs[4:9]
    mask, lap, sem = refs[9:]
    blocks, pixels, lanes = feat_hbm.shape
    slots = lists_hbm.shape[1]
    cycle = len(CYCLE_STEPS) * pixels
    device = lax.axis_index("pix")
    copies = [
        pltpu.make_async_copy(mask_hbm, mask, sem.at[0]),
        pltpu.make_async_copy(feat_hbm, value.at[:, :, pl.ds(0, lanes)], sem.at[1]),
        pltpu.make_async_copy(cot_hbm, value.at[:, :, pl.ds(lanes, lanes)], sem.at[2]),
        pltpu.make_async_copy(lap_hbm, lap, sem.at[3]),
        pltpu.make_async_copy(rows_hbm, rows_ref, sem.at[4]),
        pltpu.make_async_copy(lists_hbm, lists_ref, sem.at[5]),
    ]
    for copy in copies:
        copy.start()
    diagonal = lax.broadcasted_iota(jnp.int32, (pixels, pixels), 0) == lax.broadcasted_iota(
        jnp.int32, (pixels, pixels), 1
    )
    copies[0].wait()
    for a in range(blocks):
        row = mask[a:a + 1, :].astype(F32)
        column = jnp.sum(jnp.where(diagonal, row, 0.0), axis=1, keepdims=True)
        keep[a] = jnp.broadcast_to(column, (pixels, 2 * lanes)).astype(BF16)
    copies[1].wait()
    copies[2].wait()
    masked = [value[a] * keep[a] for a in range(blocks)]
    for a in range(blocks):
        value[a] = masked[a]
    copies[4].wait()
    copies[5].wait()
    copies[3].wait()
    for a in range(blocks):
        total = matmul(lap[a, :, :cycle], jnp.concatenate(ring_rows(value, a), axis=0))
        total = total + matmul(lap[a, :, cycle + pixels:], value[rows_ref[1, a]])
        part[a] = total * keep[a].astype(F32)
    tail = slots * 2 * pixels
    which = lax.broadcasted_iota(jnp.int32, (16, pixels), 0)
    for pairing, send in zip(ORDER, sends):
        heading = send_heading(pairing, device)
        flags = jnp.zeros((16, pixels), F32)
        for s in range(slots):
            b = lists_ref[0, s, heading]
            base = s * 2 * pixels
            send[base:base + pixels, :] = value[b]
            send[base + pixels:base + 2 * pixels, :] = part[b].astype(BF16)
            flags = jnp.where(which == s, mask[pl.ds(b, 1), :].astype(F32), flags)
        send[tail:, :] = jnp.zeros((16, 2 * lanes), BF16)
        send[tail:, :pixels] = flags.astype(BF16)


def middle_kernel(
    rows_ref, lists_ref, feat_ref, cot_ref, lap, value, keep, part, *refs,
):
    gots, (one, two, spread), sends, (sums,) = refs[:4], refs[4:7], refs[7:11], refs[11:12]
    halo, halo_part, keep_far = refs[12:]
    blocks, pixels, lanes = feat_ref.shape
    slots = lists_ref.shape[1]
    cycle = len(CYCLE_STEPS) * pixels
    flat, width = blocks * pixels, 2 * lanes
    device = lax.axis_index("pix")
    tail = slots * 2 * pixels
    for pairing, got in zip(ORDER, gots):
        heading = send_heading(pairing, device) ^ 1
        flags = got[tail:, :pixels].astype(F32)
        for s in range(slots):
            row = row_of_slot(rows_ref, heading * slots + s)
            base = s * 2 * pixels
            halo[row] = got[base:base + pixels, :]
            halo_part[row] = got[base + pixels:base + 2 * pixels, :]
            keep_far[pl.ds(row, 1), :] = flags[s:s + 1, :]
    for a in range(blocks):
        cross = lap[a, :, cycle:cycle + pixels] * keep_far[a:a + 1, :].astype(BF16)
        total = part[a] + matmul(cross, halo[a]) * keep[a].astype(F32)
        one[a] = total.astype(BF16)
        total = halo_part[a].astype(F32) + matmul_tn(cross, value[a])
        halo[a] = total.astype(BF16)
    for a in range(blocks):
        near = ring_rows(one, a) + [halo[a], one[rows_ref[1, a]]]
        total = matmul(lap[a], jnp.concatenate(near, axis=0)) * keep[a].astype(F32)
        base = jnp.concatenate([feat_ref[a], cot_ref[a]], axis=1).astype(F32)
        fresh = (2.0 * total - base).astype(BF16)
        two[a] = fresh
        spread[a] = fresh * keep[a]
    for pairing, send in zip(ORDER_TWO, sends):
        heading = send_heading(pairing, device)
        for s in range(slots):
            send[s * pixels:(s + 1) * pixels, :] = spread[lists_ref[0, s, heading]]
    feat = feat_ref[...].reshape(flat, lanes)
    cot = cot_ref[...].reshape(flat, lanes)
    first = one[...].reshape(flat, width)
    second = two[...].reshape(flat, width)
    half = lanes // 2
    low = matmul_tn(jnp.concatenate([feat, first[:, :lanes]], axis=1), cot)
    high = matmul_tn(
        jnp.concatenate([first[:, :lanes], second[:, :lanes]], axis=1), first[:, lanes:]
    )

    def trace(product, start):
        return (
            product[start:start + half, :half] + product[start + half:start + lanes, half:]
        )

    sum_zero = trace(low, 0)
    sum_one = trace(low, lanes)
    totals = jnp.concatenate(
        [
            jnp.concatenate([sum_zero, sum_one], axis=1),
            jnp.concatenate(
                [2.0 * trace(high, 0) - sum_zero, 2.0 * trace(high, lanes) - sum_one], axis=1
            ),
            jnp.broadcast_to(jnp.sum(cot.astype(F32), axis=0, keepdims=True), (16, lanes)),
        ],
        axis=0,
    )
    coarse = totals.astype(BF16)
    fine = (totals - coarse.astype(F32)).astype(BF16)
    send = sends[ORDER_TWO.index(0)]
    send[slots * pixels:, :lanes] = coarse
    send[slots * pixels:, lanes:] = fine
    sums[...] = coarse.astype(F32) + fine.astype(F32)


def partial_kernel(
    feat_ref, cot_ref, one, two, weight_hbm, bias_hbm, out_part, grad_part, mix_last,
    mix, bias_row, weight, bias, sem,
):
    blocks, pixels, lanes = feat_ref.shape
    copies = [
        pltpu.make_async_copy(weight_hbm, weight, sem.at[0]),
        pltpu.make_async_copy(bias_hbm, bias, sem.at[1]),
    ]
    for copy in copies:
        copy.start()
    for copy in copies:
        copy.wait()
    terms, half, _ = weight.shape
    mix[...] = jnp.zeros_like(mix)
    mix_last[...] = jnp.zeros_like(mix_last)
    for m in range(lanes // half):
        spot = slice(m * half, (m + 1) * half)
        for k in range(terms - 1):
            shifted = slice(k * lanes + m * half, k * lanes + (m + 1) * half)
            mix[spot, shifted] = weight[k]
        mix_last[spot, spot] = weight[terms - 1]
        bias_row[:, spot] = bias[...]
    flat = blocks * pixels
    first = one[...].reshape(flat, 2 * lanes)
    second = two[...].reshape(flat, 2 * lanes)
    total = jnp.broadcast_to(bias_row[...], (flat, lanes))
    fields = [feat_ref[...].reshape(flat, lanes), first[:, :lanes], second[:, :lanes]]
    for k, field in enumerate(fields):
        total = total + matmul(field, mix[:, k * lanes:(k + 1) * lanes])
    out_part[...] = total.reshape(blocks, pixels, lanes)
    fields = [cot_ref[...].reshape(flat, lanes), first[:, lanes:], second[:, lanes:]]
    total = matmul_nt(jnp.concatenate(fields, axis=1), mix[...])
    grad_part[...] = total.reshape(blocks, pixels, lanes)


def last_kernel(
    rows_ref, lap, keep, one, spread, out_part, grad_part, mix_last, *refs,
):
    gots, (out_ref, grad_ref), (halo, three) = refs[:4], refs[4:6], refs[6:]
    blocks, pixels, lanes = out_part.shape
    device = lax.axis_index("pix")
    slots = 2 * blocks // len(gots) // 2
    for pairing, got in zip(ORDER_TWO, gots):
        heading = send_heading(pairing, device) ^ 1
        for s in range(slots):
            row = row_of_slot(rows_ref, heading * slots + s)
            halo[row] = got[s * pixels:(s + 1) * pixels, :]
    for a in range(blocks):
        near = ring_rows(spread, a) + [halo[a], spread[rows_ref[1, a]]]
        total = matmul(lap[a], jnp.concatenate(near, axis=0)) * keep[a].astype(F32)
        three[a] = (2.0 * total - one[a].astype(F32)).astype(BF16)
    flat = blocks * pixels
    last = three[...].reshape(flat, 2 * lanes)
    total = out_part[...].reshape(flat, lanes) + matmul(last[:, :lanes], mix_last[...])
    out_ref[...] = total.astype(BF16).reshape(blocks, pixels, lanes)
    total = grad_part[...].reshape(flat, lanes) + matmul_nt(last[:, lanes:], mix_last[...])
    grad_ref[...] = total.astype(BF16).reshape(blocks, pixels, lanes)


def finish_kernel(factor, mine, other, weight_ref, bias_ref):
    sums = (mine[...] + other[...]) * factor
    terms, half, _ = weight_ref.shape
    lanes = 2 * half
    for k in range(terms):
        rows, cols = k // 2 * half, k % 2 * half
        weight_ref[k] = sums[rows:rows + half, cols:cols + half]
    bias = sums[lanes:lanes + 1, :]
    bias_ref[...] = bias[:, :half] + bias[:, half:]


def call(kernel, outs, ins, scratch, flops, hbm_from=None):
    vmem = pl.BlockSpec(memory_space=pltpu.VMEM)
    smem = pl.BlockSpec(memory_space=pltpu.SMEM)
    hbm = pl.BlockSpec(memory_space=pltpu.MemorySpace.HBM)
    touched = sum(math.prod(x.shape) * x.dtype.itemsize for x in [*ins, *outs])
    hbm_from = len(ins) if hbm_from is None else hbm_from
    ins = ins[:hbm_from] + [
        pltpu.with_memory_space_constraint(x, pltpu.MemorySpace.HBM) for x in ins[hbm_from:]
    ]

    def place(i, x):
        if i >= hbm_from:
            return hbm
        return smem if i < 2 and x.dtype == jnp.int32 else vmem

    return pl.pallas_call(
        kernel,
        out_shape=outs,
        in_specs=[place(i, x) for i, x in enumerate(ins)],
        out_specs=[smem if x.dtype == jnp.int32 else vmem for x in outs],
        scratch_shapes=scratch,
        cost_estimate=pl.CostEstimate(flops=flops, transcendentals=0, bytes_accessed=touched),
        compiler_params=pltpu.CompilerParams(vmem_limit_bytes=32 << 20),
    )(*ins)


def local(
    features, cheb_weights, out_bias, lap_tiles, neighbours, send_blocks, pixel_mask, cotangent
):
    blocks, pixels, lanes = features.shape
    terms, chan_in, chan_out = cheb_weights.shape
    slots = send_blocks.shape[2]
    width, flat = 2 * lanes, blocks * pixels
    shape = jax.ShapeDtypeStruct
    apply_flops = 2 * flat * width * lap_tiles.shape[2]
    rows = neighbours.T
    lists = send_blocks.transpose(0, 2, 1)

    field = shape((blocks, pixels, width), BF16)
    wide = shape((blocks, pixels, width), F32)
    scratch_field = pltpu.VMEM((blocks, pixels, width), BF16)
    *sends, value, keep, part, rows, lists = call(
        pack_kernel,
        [shape((slots * 2 * pixels + 16, width), BF16)] * 4 + [field, field, wide]
        + [shape(rows.shape, jnp.int32), shape(lists.shape, jnp.int32)],
        [rows, lists, pixel_mask, features, cotangent, lap_tiles],
        [
            pltpu.VMEM((blocks, pixels), jnp.int32),
            pltpu.VMEM(lap_tiles.shape, BF16),
            pltpu.SemaphoreType.DMA((6,)),
        ],
        apply_flops,
        hbm_from=0,
    )
    gots = [exchange(send, k) for k, send in zip(ORDER, sends)]
    one, two, spread, *sends, sums = call(
        middle_kernel,
        [field, field, field]
        + [
            shape((slots * pixels + (lanes + 16 if k == 0 else 0), width), BF16)
            for k in ORDER_TWO
        ]
        + [shape((lanes + 16, lanes), F32)],
        [rows, lists, features, cotangent, lap_tiles, value, keep, part, *gots],
        [scratch_field, scratch_field, pltpu.VMEM((blocks, pixels), F32)],
        2 * apply_flops,
    )
    gots = [exchange(send, k) for k, send in zip(ORDER_TWO, sends)]
    half_field = shape((blocks, pixels, lanes), F32)
    *parts, mix_last = call(
        partial_kernel,
        [half_field, half_field, shape((lanes, lanes), BF16)],
        [features, cotangent, one, two, cheb_weights, out_bias.reshape(1, chan_out)],
        [
            pltpu.VMEM((lanes, (terms - 1) * lanes), BF16),
            pltpu.VMEM((1, lanes), F32),
            pltpu.VMEM(cheb_weights.shape, BF16),
            pltpu.VMEM((1, chan_out), F32),
            pltpu.SemaphoreType.DMA((2,)),
        ],
        4 * flat * lanes * lanes * (terms - 1),
        hbm_from=4,
    )
    count = lax.axis_size("pix")
    pair = lax.axis_size("dp")
    factor = 1.0 / math.sqrt(flat * (lanes // chan_in) * count * pair)
    def swap(block, step):
        if step == 0:
            return lax.ppermute(block, "dp", [(i ^ 1, i) for i in range(pair)])
        return lax.ppermute(block, "pix", [(i ^ step, i) for i in range(count)])

    tail = gots[ORDER_TWO.index(0)][slots * pixels:].astype(F32)
    other = tail[:, :lanes] + tail[:, lanes:]
    for step in STEPS:
        sums = sums + other
        if step in TIES:
            spots = [ORDER_TWO.index(k) for k in TIES[step]]
            sums, *held = lax.optimization_barrier((sums, *[gots[i] for i in spots]))
            for i, block in zip(spots, held):
                gots[i] = block
        other = swap(sums, step)
    output_maps, grad_features = call(
        last_kernel,
        [shape(features.shape, BF16), shape(features.shape, BF16)],
        [rows, lap_tiles, keep, one, spread, *parts, mix_last, *gots],
        [scratch_field, scratch_field],
        2 * apply_flops,
    )
    grad_weights, grad_bias = call(
        functools.partial(finish_kernel, factor),
        [shape(cheb_weights.shape, F32), shape((1, chan_out), F32)],
        [sums, other],
        [],
        sums.size,
    )
    return output_maps, grad_features, grad_weights, grad_bias.reshape(chan_out)


def solution(mesh):
    return jax.shard_map(
        local,
        mesh=mesh,
        in_specs=(
            P("pix", None, ("groups", "dp")),
            P(),
            P(),
            P("pix", None, None),
            P("pix", None),
            P("pix", None, None),
            P("pix", None),
            P("pix", None, ("groups", "dp")),
        ),
        out_specs=(
            P("pix", None, ("groups", "dp")),
            P("pix", None, ("groups", "dp")),
            P("groups", None, None),
            P("groups"),
        ),
        check_vma=False,
    )
```

```python
import functools
import math

import jax
import jax.numpy as jnp
from jax import lax
from jax.experimental import pallas as pl
from jax.experimental.pallas import tpu as pltpu
from jax.sharding import PartitionSpec as P

CYCLE_STEPS = (0, -1, 1, -2, 2, -3, 3)
ORDER = (3, 1, 2, 0)
ORDER_TWO = (3, 1, 2, 0)
SPLIT = 2
OUTSIDE = 16
F32 = jnp.float32
BF16 = jnp.bfloat16


def pair_of(index, pairing, count):
    if pairing == 0:
        return index ^ 1
    if pairing == 1:
        return (index + 1 if index % 2 else index - 1) % count
    low = index % 4 < 2
    step = 2 if low == (pairing == 2) else -2
    return (index + step) % count


def exchange(block, pairing):
    count = lax.axis_size("pix")
    route = [(pair_of(i, pairing, count), i) for i in range(count)]
    return lax.ppermute(block, "pix", route)


def send_heading(pairing, device):
    if pairing < 2:
        return (device + pairing) % 2
    return 2 + (device // 2 + pairing) % 2


def matmul(left, right):
    return jnp.dot(left, right, preferred_element_type=F32)


def matmul_tn(left, right):
    return lax.dot_general(left, right, (((0,), (0,)), ((), ())), preferred_element_type=F32)


def matmul_nt(left, right):
    return lax.dot_general(left, right, (((1,), (1,)), ((), ())), preferred_element_type=F32)


def row_of_slot(rows_ref, slot):
    blocks = rows_ref.shape[1]
    found = jnp.int32(0)
    for a in range(blocks):
        found = jnp.where(rows_ref[0, a] == blocks + slot, a, found)
    return found


def ring_rows(field, a):
    blocks = field.shape[0]
    return [field[(a + step) % blocks] for step in CYCLE_STEPS]


def pack_kernel(
    rows_hbm, lists_hbm, mask_hbm, feat_hbm, cot_hbm, lap_hbm,
    *refs,
):
    sends, (value, keep, part, rows_ref, lists_ref) = refs[:4], refs[4:9]
    mask, lap, sem = refs[9:]
    blocks, pixels, lanes = feat_hbm.shape
    slots = lists_hbm.shape[1]
    cycle = len(CYCLE_STEPS) * pixels
    device = lax.axis_index("pix")
    copies = [
        pltpu.make_async_copy(mask_hbm, mask, sem.at[0]),
        pltpu.make_async_copy(feat_hbm, value.at[:, :, pl.ds(0, lanes)], sem.at[1]),
        pltpu.make_async_copy(cot_hbm, value.at[:, :, pl.ds(lanes, lanes)], sem.at[2]),
        pltpu.make_async_copy(lap_hbm, lap, sem.at[3]),
        pltpu.make_async_copy(rows_hbm, rows_ref, sem.at[4]),
        pltpu.make_async_copy(lists_hbm, lists_ref, sem.at[5]),
    ]
    for copy in copies:
        copy.start()
    diagonal = lax.broadcasted_iota(jnp.int32, (pixels, pixels), 0) == lax.broadcasted_iota(
        jnp.int32, (pixels, pixels), 1
    )
    copies[0].wait()
    for a in range(blocks):
        row = mask[a:a + 1, :].astype(F32)
        column = jnp.sum(jnp.where(diagonal, row, 0.0), axis=1, keepdims=True)
        keep[a] = jnp.broadcast_to(column, (pixels, 2 * lanes)).astype(BF16)
    copies[1].wait()
    copies[2].wait()
    masked = [value[a] * keep[a] for a in range(blocks)]
    for a in range(blocks):
        value[a] = masked[a]
    copies[4].wait()
    copies[5].wait()
    copies[3].wait()
    for a in range(blocks):
        total = matmul(lap[a, :, :cycle], jnp.concatenate(ring_rows(value, a), axis=0))
        total = total + matmul(lap[a, :, cycle + pixels:], value[rows_ref[1, a]])
        part[a] = total * keep[a].astype(F32)
    for pairing, send in zip(ORDER, sends):
        heading = send_heading(pairing, device)
        for s in range(slots):
            b = lists_ref[0, s, heading]
            base = s * 2 * pixels
            send[base:base + pixels, :] = value[b] + (1 - keep[b]) * OUTSIDE
            send[base + pixels:base + 2 * pixels, :] = part[b].astype(BF16)


def middle_kernel(
    rows_ref, lists_ref, feat_ref, cot_ref, lap, value, keep, part, *refs,
):
    gots, (one, two, spread), sends, (sums,) = refs[:4], refs[4:7], refs[7:11], refs[11:12]
    halo, halo_part, keep_far = refs[12:]
    blocks, pixels, lanes = feat_ref.shape
    slots = lists_ref.shape[1]
    cycle = len(CYCLE_STEPS) * pixels
    flat, width = blocks * pixels, 2 * lanes
    device = lax.axis_index("pix")
    for pairing, got in zip(ORDER, gots):
        heading = send_heading(pairing, device) ^ 1
        for s in range(slots):
            row = row_of_slot(rows_ref, heading * slots + s)
            base = s * 2 * pixels
            arrived = got[base:base + pixels, :].astype(F32)
            outside = arrived > OUTSIDE / 2
            halo[row] = jnp.where(outside, 0.0, arrived).astype(BF16)
            keep_far[row] = jnp.where(outside, 0.0, 1.0).astype(BF16)
            halo_part[row] = got[base + pixels:base + 2 * pixels, :]
    for a in range(blocks):
        cross = lap[a, :, cycle:cycle + pixels]
        total = part[a] + matmul(cross, halo[a]) * keep[a].astype(F32)
        one[a] = total.astype(BF16)
        total = halo_part[a].astype(F32) + matmul_tn(cross, value[a]) * keep_far[a].astype(F32)
        halo[a] = total.astype(BF16)
    for a in range(blocks):
        near = ring_rows(one, a) + [halo[a], one[rows_ref[1, a]]]
        total = matmul(lap[a], jnp.concatenate(near, axis=0)) * keep[a].astype(F32)
        base = jnp.concatenate([feat_ref[a], cot_ref[a]], axis=1).astype(F32)
        fresh = (2.0 * total - base).astype(BF16)
        two[a] = fresh
        spread[a] = fresh * keep[a]
    for pairing, send in zip(ORDER_TWO, sends):
        heading = send_heading(pairing, device)
        for s in range(slots):
            send[s * pixels:(s + 1) * pixels, :] = spread[lists_ref[0, s, heading]]
    feat = feat_ref[...].reshape(flat, lanes)
    cot = cot_ref[...].reshape(flat, lanes)
    first = one[...].reshape(flat, width)
    second = two[...].reshape(flat, width)
    half = lanes // 2
    low = matmul_tn(jnp.concatenate([feat, first[:, :lanes]], axis=1), cot)
    high = matmul_tn(
        jnp.concatenate([first[:, :lanes], second[:, :lanes]], axis=1), first[:, lanes:]
    )

    def trace(product, start):
        return (
            product[start:start + half, :half] + product[start + half:start + lanes, half:]
        )

    sum_zero = trace(low, 0)
    sum_one = trace(low, lanes)
    totals = jnp.concatenate(
        [
            jnp.concatenate([sum_zero, sum_one], axis=1),
            jnp.concatenate(
                [2.0 * trace(high, 0) - sum_zero, 2.0 * trace(high, lanes) - sum_one], axis=1
            ),
            jnp.broadcast_to(jnp.sum(cot.astype(F32), axis=0, keepdims=True), (8, lanes)),
        ],
        axis=0,
    )
    sums[...] = totals


def partial_kernel(
    feat_ref, cot_ref, one, two, weight_hbm, bias_hbm, out_part, grad_part, mix_last,
    mix, bias_row, weight, bias, sem,
):
    blocks, pixels, lanes = feat_ref.shape
    copies = [
        pltpu.make_async_copy(weight_hbm, weight, sem.at[0]),
        pltpu.make_async_copy(bias_hbm, bias, sem.at[1]),
    ]
    for copy in copies:
        copy.start()
    for copy in copies:
        copy.wait()
    terms, half, _ = weight.shape
    mix[...] = jnp.zeros_like(mix)
    mix_last[...] = jnp.zeros_like(mix_last)
    for m in range(lanes // half):
        spot = slice(m * half, (m + 1) * half)
        for k in range(terms - 1):
            shifted = slice(k * lanes + m * half, k * lanes + (m + 1) * half)
            mix[spot, shifted] = weight[k]
        mix_last[spot, spot] = weight[terms - 1]
        bias_row[:, spot] = bias[...]
    flat = blocks * pixels
    first = one[...].reshape(flat, 2 * lanes)
    second = two[...].reshape(flat, 2 * lanes)
    total = jnp.broadcast_to(bias_row[...], (flat, lanes))
    fields = [feat_ref[...].reshape(flat, lanes), first[:, :lanes], second[:, :lanes]]
    for k, field in enumerate(fields):
        total = total + matmul(field, mix[:, k * lanes:(k + 1) * lanes])
    out_part[...] = total.reshape(blocks, pixels, lanes)
    fields = [cot_ref[...].reshape(flat, lanes), first[:, lanes:], second[:, lanes:]]
    total = matmul_nt(jnp.concatenate(fields, axis=1), mix[...])
    grad_part[...] = total.reshape(blocks, pixels, lanes)


def last_kernel(
    rows_ref, lap, keep, one, spread, out_part, grad_part, mix_last, *refs,
):
    gots, (out_hbm, grad_hbm), (halo, three, out_ref, grad_ref, sem) = refs[:4], refs[4:6], refs[6:]
    blocks, pixels, lanes = out_part.shape
    device = lax.axis_index("pix")
    slots = gots[0].shape[0] // pixels
    for pairing, got in zip(ORDER_TWO, gots):
        heading = send_heading(pairing, device) ^ 1
        for s in range(slots):
            row = row_of_slot(rows_ref, heading * slots + s)
            halo[row] = got[s * pixels:(s + 1) * pixels, :]
    group = blocks // SPLIT
    size = group * pixels
    copies = []
    for start in range(0, blocks, group):
        for a in range(start, start + group):
            near = ring_rows(spread, a) + [halo[a], spread[rows_ref[1, a]]]
            total = matmul(lap[a], jnp.concatenate(near, axis=0)) * keep[a].astype(F32)
            three[a] = (2.0 * total - one[a].astype(F32)).astype(BF16)
        mine = pl.ds(start, group)
        last = three[mine].reshape(size, 2 * lanes)
        total = out_part[mine].reshape(size, lanes) + matmul(last[:, :lanes], mix_last[...])
        out_ref[mine] = total.astype(BF16).reshape(group, pixels, lanes)
        total = grad_part[mine].reshape(size, lanes) + matmul_nt(last[:, lanes:], mix_last[...])
        grad_ref[mine] = total.astype(BF16).reshape(group, pixels, lanes)
        for source, target in ((out_ref, out_hbm), (grad_ref, grad_hbm)):
            copies.append(
                pltpu.make_async_copy(source.at[mine], target.at[mine], sem.at[len(copies)])
            )
            copies[-1].start()
    for copy in copies:
        copy.wait()


def finish_kernel(factor, mine, other, weight_ref, bias_ref):
    sums = (mine[...] + other[...]) * factor
    terms, half, _ = weight_ref.shape
    lanes = 2 * half
    for k in range(terms):
        rows, cols = k // 2 * half, k % 2 * half
        weight_ref[k] = sums[rows:rows + half, cols:cols + half]
    bias = sums[lanes:lanes + 1, :]
    bias_ref[...] = bias[:, :half] + bias[:, half:]


def call(kernel, outs, ins, scratch, flops, hbm_from=None, out_hbm=False):
    vmem = pl.BlockSpec(memory_space=pltpu.VMEM)
    smem = pl.BlockSpec(memory_space=pltpu.SMEM)
    hbm = pl.BlockSpec(memory_space=pltpu.MemorySpace.HBM)
    touched = sum(math.prod(x.shape) * x.dtype.itemsize for x in [*ins, *outs])
    hbm_from = len(ins) if hbm_from is None else hbm_from
    ins = ins[:hbm_from] + [
        pltpu.with_memory_space_constraint(x, pltpu.MemorySpace.HBM) for x in ins[hbm_from:]
    ]

    def place(i, x):
        if i >= hbm_from:
            return hbm
        return smem if i < 2 and x.dtype == jnp.int32 else vmem

    return pl.pallas_call(
        kernel,
        out_shape=outs,
        in_specs=[place(i, x) for i, x in enumerate(ins)],
        out_specs=[hbm if out_hbm else smem if x.dtype == jnp.int32 else vmem for x in outs],
        scratch_shapes=scratch,
        cost_estimate=pl.CostEstimate(flops=flops, transcendentals=0, bytes_accessed=touched),
        compiler_params=pltpu.CompilerParams(vmem_limit_bytes=32 << 20),
    )(*ins)


def local(
    features, cheb_weights, out_bias, lap_tiles, neighbours, send_blocks, pixel_mask, cotangent
):
    blocks, pixels, lanes = features.shape
    terms, chan_in, chan_out = cheb_weights.shape
    slots = send_blocks.shape[2]
    width, flat = 2 * lanes, blocks * pixels
    shape = jax.ShapeDtypeStruct
    apply_flops = 2 * flat * width * lap_tiles.shape[2]
    rows = neighbours.T
    lists = send_blocks.transpose(0, 2, 1)

    field = shape((blocks, pixels, width), BF16)
    wide = shape((blocks, pixels, width), F32)
    scratch_field = pltpu.VMEM((blocks, pixels, width), BF16)
    *sends, value, keep, part, rows, lists = call(
        pack_kernel,
        [shape((slots * 2 * pixels, width), BF16)] * 4 + [field, field, wide]
        + [shape(rows.shape, jnp.int32), shape(lists.shape, jnp.int32)],
        [rows, lists, pixel_mask, features, cotangent, lap_tiles],
        [
            pltpu.VMEM((blocks, pixels), jnp.int32),
            pltpu.VMEM(lap_tiles.shape, BF16),
            pltpu.SemaphoreType.DMA((6,)),
        ],
        apply_flops,
        hbm_from=0,
    )
    gots = [exchange(send, k) for k, send in zip(ORDER, sends)]
    one, two, spread, *sends, sums = call(
        middle_kernel,
        [field, field, field]
        + [shape((slots * pixels, width), BF16)] * 4
        + [shape((lanes + 8, lanes), F32)],
        [rows, lists, features, cotangent, lap_tiles, value, keep, part, *gots],
        [scratch_field, scratch_field, scratch_field],
        2 * apply_flops,
    )
    gots = [exchange(send, k) for k, send in zip(ORDER_TWO, sends)]
    half_field = shape((blocks, pixels, lanes), F32)
    *parts, mix_last = call(
        partial_kernel,
        [half_field, half_field, shape((lanes, lanes), BF16)],
        [features, cotangent, one, two, cheb_weights, out_bias.reshape(1, chan_out)],
        [
            pltpu.VMEM((lanes, (terms - 1) * lanes), BF16),
            pltpu.VMEM((1, lanes), F32),
            pltpu.VMEM(cheb_weights.shape, BF16),
            pltpu.VMEM((1, chan_out), F32),
            pltpu.SemaphoreType.DMA((2,)),
        ],
        4 * flat * lanes * lanes * (terms - 1),
        hbm_from=4,
    )
    count = lax.axis_size("pix")
    pair = lax.axis_size("dp")
    factor = 1.0 / math.sqrt(flat * (lanes // chan_in) * count * pair)

    def swap(block, reach):
        return lax.ppermute(block, "pix", [(i ^ reach, i) for i in range(count)])

    beside = lax.ppermute(sums, "dp", [(i ^ 1, i) for i in range(pair)])
    across = lax.ppermute(
        sums, ("pix", "dp"), [(i ^ (pair + 1), i) for i in range(count * pair)]
    )
    other = swap(sums, 1) + across
    sums = sums + beside
    reach = 2
    while reach < count:
        sums = sums + other
        other = swap(sums, reach)
        reach *= 2
    output_maps, grad_features = call(
        last_kernel,
        [shape(features.shape, BF16), shape(features.shape, BF16)],
        [rows, lap_tiles, keep, one, spread, *parts, mix_last, *gots],
        [scratch_field, scratch_field]
        + [pltpu.VMEM(features.shape, BF16)] * 2
        + [pltpu.SemaphoreType.DMA((2 * SPLIT,))],
        2 * apply_flops,
        out_hbm=True,
    )
    grad_weights, grad_bias = call(
        functools.partial(finish_kernel, factor),
        [shape(cheb_weights.shape, F32), shape((1, chan_out), F32)],
        [sums, other],
        [],
        sums.size,
    )
    return output_maps, grad_features, grad_weights, grad_bias.reshape(chan_out)


def solution(mesh):
    return jax.shard_map(
        local,
        mesh=mesh,
        in_specs=(
            P("pix", None, ("groups", "dp")),
            P(),
            P(),
            P("pix", None, None),
            P("pix", None),
            P("pix", None, None),
            P("pix", None),
            P("pix", None, ("groups", "dp")),
        ),
        out_specs=(
            P("pix", None, ("groups", "dp")),
            P("pix", None, ("groups", "dp")),
            P("groups", None, None),
            P("groups"),
        ),
        check_vma=False,
    )
```

```python
import functools
import math

import jax
import jax.numpy as jnp
from jax import lax
from jax.experimental import pallas as pl
from jax.experimental.pallas import tpu as pltpu
from jax.sharding import PartitionSpec as P

CYCLE_STEPS = (0, -1, 1, -2, 2, -3, 3)
ORDER = (3, 1, 2, 0)
ORDER_TWO = (3, 1, 2, 0)
SPLIT = 2
OUTSIDE = 16
F32 = jnp.float32
BF16 = jnp.bfloat16


def pair_of(index, pairing, count):
    if pairing == 0:
        return index ^ 1
    if pairing == 1:
        return (index + 1 if index % 2 else index - 1) % count
    low = index % 4 < 2
    step = 2 if low == (pairing == 2) else -2
    return (index + step) % count


def exchange(block, pairing):
    count = lax.axis_size("pix")
    route = [(pair_of(i, pairing, count), i) for i in range(count)]
    return lax.ppermute(block, "pix", route)


def send_heading(pairing, device):
    if pairing < 2:
        return (device + pairing) % 2
    return 2 + (device // 2 + pairing) % 2


def matmul(left, right):
    return jnp.dot(left, right, preferred_element_type=F32)


def matmul_tn(left, right):
    return lax.dot_general(left, right, (((0,), (0,)), ((), ())), preferred_element_type=F32)


def matmul_nt(left, right):
    return lax.dot_general(left, right, (((1,), (1,)), ((), ())), preferred_element_type=F32)


def row_of_slot(rows_ref, slot):
    blocks = rows_ref.shape[1]
    found = jnp.int32(0)
    for a in range(blocks):
        found = jnp.where(rows_ref[0, a] == blocks + slot, a, found)
    return found


def ring_rows(field, a):
    blocks = field.shape[0]
    return [field[(a + step) % blocks] for step in CYCLE_STEPS]


def pack_kernel(
    rows_hbm, lists_hbm, mask_hbm, feat_hbm, cot_hbm, lap_hbm,
    *refs,
):
    sends, (value, keep, part, rows_ref, lists_ref) = refs[:4], refs[4:9]
    mask, lap, sem = refs[9:]
    blocks, pixels, lanes = feat_hbm.shape
    slots = lists_hbm.shape[1]
    cycle = len(CYCLE_STEPS) * pixels
    device = lax.axis_index("pix")
    copies = [
        pltpu.make_async_copy(mask_hbm, mask, sem.at[0]),
        pltpu.make_async_copy(feat_hbm, value.at[:, :, pl.ds(0, lanes)], sem.at[1]),
        pltpu.make_async_copy(cot_hbm, value.at[:, :, pl.ds(lanes, lanes)], sem.at[2]),
        pltpu.make_async_copy(lap_hbm, lap, sem.at[3]),
        pltpu.make_async_copy(rows_hbm, rows_ref, sem.at[4]),
        pltpu.make_async_copy(lists_hbm, lists_ref, sem.at[5]),
    ]
    for copy in copies:
        copy.start()
    diagonal = lax.broadcasted_iota(jnp.int32, (pixels, pixels), 0) == lax.broadcasted_iota(
        jnp.int32, (pixels, pixels), 1
    )
    copies[0].wait()
    for a in range(blocks):
        row = mask[a:a + 1, :].astype(F32)
        column = jnp.sum(jnp.where(diagonal, row, 0.0), axis=1, keepdims=True)
        keep[a] = jnp.broadcast_to(column, (pixels, 2 * lanes)).astype(BF16)
    copies[1].wait()
    copies[2].wait()
    masked = [value[a] * keep[a] for a in range(blocks)]
    for a in range(blocks):
        value[a] = masked[a]
    copies[4].wait()
    copies[5].wait()
    copies[3].wait()
    for a in range(blocks):
        total = matmul(lap[a, :, :cycle], jnp.concatenate(ring_rows(value, a), axis=0))
        total = total + matmul(lap[a, :, cycle + pixels:], value[rows_ref[1, a]])
        part[a] = total * keep[a].astype(F32)
    for pairing, send in zip(ORDER, sends):
        heading = send_heading(pairing, device)
        for s in range(slots):
            b = lists_ref[0, s, heading]
            base = s * 2 * pixels
            send[base:base + pixels, :] = value[b] + (1 - keep[b]) * OUTSIDE
            send[base + pixels:base + 2 * pixels, :] = part[b].astype(BF16)


def early_kernel(
    feat_ref, cot_ref, lap, value, weight_hbm, bias_hbm,
    turned, zero_sums, mix, mix_last, bias_row,
    weight, bias, sem,
):
    blocks, pixels, lanes = feat_ref.shape
    cycle = len(CYCLE_STEPS) * pixels
    copies = [
        pltpu.make_async_copy(weight_hbm, weight, sem.at[0]),
        pltpu.make_async_copy(bias_hbm, bias, sem.at[1]),
    ]
    for copy in copies:
        copy.start()
    for a in range(blocks):
        turned[a] = matmul_tn(lap[a, :, cycle:cycle + pixels], value[a])
    feat = feat_ref[...].reshape(blocks * pixels, lanes)
    cot = cot_ref[...].reshape(blocks * pixels, lanes)
    zero_sums[:lanes, :] = matmul_tn(feat, cot)
    zero_sums[lanes:, :] = jnp.broadcast_to(
        jnp.sum(cot.astype(F32), axis=0, keepdims=True), (8, lanes)
    )
    for copy in copies:
        copy.wait()
    terms, half, _ = weight.shape
    mix[...] = jnp.zeros_like(mix)
    mix_last[...] = jnp.zeros_like(mix_last)
    for m in range(lanes // half):
        spot = slice(m * half, (m + 1) * half)
        for k in range(terms - 1):
            shifted = slice(k * lanes + m * half, k * lanes + (m + 1) * half)
            mix[spot, shifted] = weight[k]
        mix_last[spot, spot] = weight[terms - 1]
        bias_row[:, spot] = bias[...]


def middle_kernel(
    rows_ref, lists_ref, feat_ref, cot_ref, lap, keep, part, turned, zero_sums, *refs,
):
    gots, (one, two, spread), sends, (sums,) = refs[:4], refs[4:7], refs[7:11], refs[11:12]
    halo, halo_part, keep_far = refs[12:]
    blocks, pixels, lanes = feat_ref.shape
    slots = lists_ref.shape[1]
    cycle = len(CYCLE_STEPS) * pixels
    flat, width = blocks * pixels, 2 * lanes
    device = lax.axis_index("pix")
    for pairing, got in zip(ORDER, gots):
        heading = send_heading(pairing, device) ^ 1
        for s in range(slots):
            row = row_of_slot(rows_ref, heading * slots + s)
            base = s * 2 * pixels
            arrived = got[base:base + pixels, :].astype(F32)
            outside = arrived > OUTSIDE / 2
            halo[row] = jnp.where(outside, 0.0, arrived).astype(BF16)
            keep_far[row] = jnp.where(outside, 0.0, 1.0).astype(BF16)
            halo_part[row] = got[base + pixels:base + 2 * pixels, :]
    for a in range(blocks):
        cross = lap[a, :, cycle:cycle + pixels]
        total = part[a] + matmul(cross, halo[a]) * keep[a].astype(F32)
        one[a] = total.astype(BF16)
        total = halo_part[a].astype(F32) + turned[a] * keep_far[a].astype(F32)
        halo[a] = total.astype(BF16)
    for a in range(blocks):
        near = ring_rows(one, a) + [halo[a], one[rows_ref[1, a]]]
        total = matmul(lap[a], jnp.concatenate(near, axis=0)) * keep[a].astype(F32)
        base = jnp.concatenate([feat_ref[a], cot_ref[a]], axis=1).astype(F32)
        fresh = (2.0 * total - base).astype(BF16)
        two[a] = fresh
        spread[a] = fresh * keep[a]
    for pairing, send in zip(ORDER_TWO, sends):
        heading = send_heading(pairing, device)
        for s in range(slots):
            send[s * pixels:(s + 1) * pixels, :] = spread[lists_ref[0, s, heading]]
    cot = cot_ref[...].reshape(flat, lanes)
    first = one[...].reshape(flat, width)
    second = two[...].reshape(flat, width)
    half = lanes // 2
    low = matmul_tn(first[:, :lanes], cot)
    high = matmul_tn(
        jnp.concatenate([first[:, :lanes], second[:, :lanes]], axis=1), first[:, lanes:]
    )

    def trace(product, start):
        return (
            product[start:start + half, :half] + product[start + half:start + lanes, half:]
        )

    sum_zero = trace(zero_sums, 0)
    sum_one = trace(low, 0)
    totals = jnp.concatenate(
        [
            jnp.concatenate([sum_zero, sum_one], axis=1),
            jnp.concatenate(
                [2.0 * trace(high, 0) - sum_zero, 2.0 * trace(high, lanes) - sum_one], axis=1
            ),
            zero_sums[lanes:, :],
        ],
        axis=0,
    )
    sums[...] = totals


def partial_kernel(
    rows_ref, feat_ref, cot_ref, lap, keep, one, two, spread, mix, bias_row,
    out_part, grad_part, three_part,
):
    blocks, pixels, lanes = feat_ref.shape
    cycle = len(CYCLE_STEPS) * pixels
    for a in range(blocks):
        total = matmul(lap[a, :, :cycle], jnp.concatenate(ring_rows(spread, a), axis=0))
        total = total + matmul(lap[a, :, cycle + pixels:], spread[rows_ref[1, a]])
        three_part[a] = 2.0 * total * keep[a].astype(F32) - one[a].astype(F32)
    flat = blocks * pixels
    first = one[...].reshape(flat, 2 * lanes)
    second = two[...].reshape(flat, 2 * lanes)
    total = jnp.broadcast_to(bias_row[...], (flat, lanes))
    fields = [feat_ref[...].reshape(flat, lanes), first[:, :lanes], second[:, :lanes]]
    for k, field in enumerate(fields):
        total = total + matmul(field, mix[:, k * lanes:(k + 1) * lanes])
    out_part[...] = total.reshape(blocks, pixels, lanes)
    fields = [cot_ref[...].reshape(flat, lanes), first[:, lanes:], second[:, lanes:]]
    total = matmul_nt(jnp.concatenate(fields, axis=1), mix[...])
    grad_part[...] = total.reshape(blocks, pixels, lanes)


def last_kernel(
    rows_ref, lap, keep, out_part, grad_part, three_part, mix_last, *refs,
):
    gots, (out_hbm, grad_hbm), (halo, three, out_ref, grad_ref, sem) = refs[:4], refs[4:6], refs[6:]
    blocks, pixels, lanes = out_part.shape
    device = lax.axis_index("pix")
    slots = gots[0].shape[0] // pixels
    for pairing, got in zip(ORDER_TWO, gots):
        heading = send_heading(pairing, device) ^ 1
        for s in range(slots):
            row = row_of_slot(rows_ref, heading * slots + s)
            halo[row] = got[s * pixels:(s + 1) * pixels, :]
    cycle = len(CYCLE_STEPS) * pixels
    group = blocks // SPLIT
    size = group * pixels
    copies = []
    for start in range(0, blocks, group):
        for a in range(start, start + group):
            total = matmul(lap[a, :, cycle:cycle + pixels], halo[a]) * keep[a].astype(F32)
            three[a] = (three_part[a] + 2.0 * total).astype(BF16)
        mine = pl.ds(start, group)
        last = three[mine].reshape(size, 2 * lanes)
        total = out_part[mine].reshape(size, lanes) + matmul(last[:, :lanes], mix_last[...])
        out_ref[mine] = total.astype(BF16).reshape(group, pixels, lanes)
        total = grad_part[mine].reshape(size, lanes) + matmul_nt(last[:, lanes:], mix_last[...])
        grad_ref[mine] = total.astype(BF16).reshape(group, pixels, lanes)
        for source, target in ((out_ref, out_hbm), (grad_ref, grad_hbm)):
            copies.append(
                pltpu.make_async_copy(source.at[mine], target.at[mine], sem.at[len(copies)])
            )
            copies[-1].start()
    for copy in copies:
        copy.wait()


def finish_kernel(factor, mine, other, weight_ref, bias_ref):
    sums = (mine[...] + other[...]) * factor
    terms, half, _ = weight_ref.shape
    lanes = 2 * half
    for k in range(terms):
        rows, cols = k // 2 * half, k % 2 * half
        weight_ref[k] = sums[rows:rows + half, cols:cols + half]
    bias = sums[lanes:lanes + 1, :]
    bias_ref[...] = bias[:, :half] + bias[:, half:]


def call(kernel, outs, ins, scratch, flops, hbm_from=None, out_hbm=False):
    vmem = pl.BlockSpec(memory_space=pltpu.VMEM)
    smem = pl.BlockSpec(memory_space=pltpu.SMEM)
    hbm = pl.BlockSpec(memory_space=pltpu.MemorySpace.HBM)
    touched = sum(math.prod(x.shape) * x.dtype.itemsize for x in [*ins, *outs])
    hbm_from = len(ins) if hbm_from is None else hbm_from
    ins = ins[:hbm_from] + [
        pltpu.with_memory_space_constraint(x, pltpu.MemorySpace.HBM) for x in ins[hbm_from:]
    ]

    def place(i, x):
        if i >= hbm_from:
            return hbm
        return smem if i < 2 and x.dtype == jnp.int32 else vmem

    return pl.pallas_call(
        kernel,
        out_shape=outs,
        in_specs=[place(i, x) for i, x in enumerate(ins)],
        out_specs=[hbm if out_hbm else smem if x.dtype == jnp.int32 else vmem for x in outs],
        scratch_shapes=scratch,
        cost_estimate=pl.CostEstimate(flops=flops, transcendentals=0, bytes_accessed=touched),
        compiler_params=pltpu.CompilerParams(vmem_limit_bytes=32 << 20),
    )(*ins)


def local(
    features, cheb_weights, out_bias, lap_tiles, neighbours, send_blocks, pixel_mask, cotangent
):
    blocks, pixels, lanes = features.shape
    terms, chan_in, chan_out = cheb_weights.shape
    slots = send_blocks.shape[2]
    width, flat = 2 * lanes, blocks * pixels
    shape = jax.ShapeDtypeStruct
    apply_flops = 2 * flat * width * lap_tiles.shape[2]
    rows = neighbours.T
    lists = send_blocks.transpose(0, 2, 1)

    field = shape((blocks, pixels, width), BF16)
    wide = shape((blocks, pixels, width), F32)
    scratch_field = pltpu.VMEM((blocks, pixels, width), BF16)
    *sends, value, keep, part, rows, lists = call(
        pack_kernel,
        [shape((slots * 2 * pixels, width), BF16)] * 4 + [field, field, wide]
        + [shape(rows.shape, jnp.int32), shape(lists.shape, jnp.int32)],
        [rows, lists, pixel_mask, features, cotangent, lap_tiles],
        [
            pltpu.VMEM((blocks, pixels), jnp.int32),
            pltpu.VMEM(lap_tiles.shape, BF16),
            pltpu.SemaphoreType.DMA((6,)),
        ],
        apply_flops,
        hbm_from=0,
    )
    gots = [exchange(send, k) for k, send in zip(ORDER, sends)]
    *early, mix, mix_last, bias_row = call(
        early_kernel,
        [wide, shape((lanes + 8, lanes), F32)]
        + [shape((lanes, (terms - 1) * lanes), BF16), shape((lanes, lanes), BF16)]
        + [shape((1, lanes), F32)],
        [features, cotangent, lap_tiles, value, cheb_weights, out_bias.reshape(1, chan_out)],
        [
            pltpu.VMEM(cheb_weights.shape, BF16),
            pltpu.VMEM((1, chan_out), F32),
            pltpu.SemaphoreType.DMA((2,)),
        ],
        2 * flat * (width * pixels + lanes * lanes),
        hbm_from=4,
    )
    one, two, spread, *sends, sums = call(
        middle_kernel,
        [field, field, field]
        + [shape((slots * pixels, width), BF16)] * 4
        + [shape((lanes + 8, lanes), F32)],
        [rows, lists, features, cotangent, lap_tiles, keep, part, *early, *gots],
        [scratch_field, scratch_field, scratch_field],
        2 * apply_flops,
    )
    gots = [exchange(send, k) for k, send in zip(ORDER_TWO, sends)]
    half_field = shape((blocks, pixels, lanes), F32)
    parts = call(
        partial_kernel,
        [half_field, half_field, wide],
        [rows, features, cotangent, lap_tiles, keep, one, two, spread]
        + [mix, bias_row],
        [],
        apply_flops + 4 * flat * lanes * lanes * (terms - 1),
    )
    count = lax.axis_size("pix")
    pair = lax.axis_size("dp")
    factor = 1.0 / math.sqrt(flat * (lanes // chan_in) * count * pair)

    def swap(block, reach):
        return lax.ppermute(block, "pix", [(i ^ reach, i) for i in range(count)])

    beside = lax.ppermute(sums, "dp", [(i ^ 1, i) for i in range(pair)])
    across = lax.ppermute(
        sums, ("pix", "dp"), [(i ^ (pair + 1), i) for i in range(count * pair)]
    )
    other = swap(sums, 1) + across
    sums = sums + beside
    reach = 2
    while reach < count:
        sums = sums + other
        other = swap(sums, reach)
        reach *= 2
    output_maps, grad_features = call(
        last_kernel,
        [shape(features.shape, BF16), shape(features.shape, BF16)],
        [rows, lap_tiles, keep, *parts, mix_last, *gots],
        [scratch_field, scratch_field]
        + [pltpu.VMEM(features.shape, BF16)] * 2
        + [pltpu.SemaphoreType.DMA((2 * SPLIT,))],
        apply_flops,
        out_hbm=True,
    )
    grad_weights, grad_bias = call(
        functools.partial(finish_kernel, factor),
        [shape(cheb_weights.shape, F32), shape((1, chan_out), F32)],
        [sums, other],
        [],
        sums.size,
    )
    return output_maps, grad_features, grad_weights, grad_bias.reshape(chan_out)


def solution(mesh):
    return jax.shard_map(
        local,
        mesh=mesh,
        in_specs=(
            P("pix", None, ("groups", "dp")),
            P(),
            P(),
            P("pix", None, None),
            P("pix", None),
            P("pix", None, None),
            P("pix", None),
            P("pix", None, ("groups", "dp")),
        ),
        out_specs=(
            P("pix", None, ("groups", "dp")),
            P("pix", None, ("groups", "dp")),
            P("groups", None, None),
            P("groups"),
        ),
        check_vma=False,
    )
```

```python
import functools
import math

import jax
import jax.numpy as jnp
from jax import lax
from jax.experimental import pallas as pl
from jax.experimental.pallas import tpu as pltpu
from jax.sharding import PartitionSpec as P

CYCLE_STEPS = (0, -1, 1, -2, 2, -3, 3)
ORDER = (3, 1, 2, 0)
ORDER_TWO = (3, 1, 2, 0)
SPLIT = 1
OUTSIDE = 16
F32 = jnp.float32
BF16 = jnp.bfloat16


def pair_of(index, pairing, count):
    if pairing == 0:
        return index ^ 1
    if pairing == 1:
        return (index + 1 if index % 2 else index - 1) % count
    low = index % 4 < 2
    step = 2 if low == (pairing == 2) else -2
    return (index + step) % count


def exchange(block, pairing):
    count = lax.axis_size("pix")
    route = [(pair_of(i, pairing, count), i) for i in range(count)]
    return lax.ppermute(block, "pix", route)


def send_heading(pairing, device):
    if pairing < 2:
        return (device + pairing) % 2
    return 2 + (device // 2 + pairing) % 2


def matmul(left, right):
    return jnp.dot(left, right, preferred_element_type=F32)


def matmul_tn(left, right):
    return lax.dot_general(left, right, (((0,), (0,)), ((), ())), preferred_element_type=F32)


def matmul_nt(left, right):
    return lax.dot_general(left, right, (((1,), (1,)), ((), ())), preferred_element_type=F32)


def row_of_slot(rows_ref, slot):
    blocks = rows_ref.shape[1]
    found = jnp.int32(0)
    for a in range(blocks):
        found = jnp.where(rows_ref[0, a] == blocks + slot, a, found)
    return found


def ring_rows(field, a):
    blocks = field.shape[0]
    return [field[(a + step) % blocks] for step in CYCLE_STEPS]


def pack_kernel(
    rows_hbm, lists_hbm, mask_hbm, feat_hbm, cot_hbm, lap_hbm,
    *refs,
):
    sends, (value, keep, part, rows_ref, lists_ref) = refs[:4], refs[4:9]
    mask, lap, sem = refs[9:]
    blocks, pixels, lanes = feat_hbm.shape
    slots = lists_hbm.shape[1]
    cycle = len(CYCLE_STEPS) * pixels
    device = lax.axis_index("pix")
    copies = [
        pltpu.make_async_copy(mask_hbm, mask, sem.at[0]),
        pltpu.make_async_copy(feat_hbm, value.at[:, :, pl.ds(0, lanes)], sem.at[1]),
        pltpu.make_async_copy(cot_hbm, value.at[:, :, pl.ds(lanes, lanes)], sem.at[2]),
        pltpu.make_async_copy(lap_hbm, lap, sem.at[3]),
        pltpu.make_async_copy(rows_hbm, rows_ref, sem.at[4]),
        pltpu.make_async_copy(lists_hbm, lists_ref, sem.at[5]),
    ]
    for copy in copies:
        copy.start()
    diagonal = lax.broadcasted_iota(jnp.int32, (pixels, pixels), 0) == lax.broadcasted_iota(
        jnp.int32, (pixels, pixels), 1
    )
    copies[0].wait()
    for a in range(blocks):
        row = mask[a:a + 1, :].astype(F32)
        column = jnp.sum(jnp.where(diagonal, row, 0.0), axis=1, keepdims=True)
        keep[a] = jnp.broadcast_to(column, (pixels, 2 * lanes)).astype(BF16)
    copies[1].wait()
    copies[2].wait()
    masked = [value[a] * keep[a] for a in range(blocks)]
    for a in range(blocks):
        value[a] = masked[a]
    copies[4].wait()
    copies[5].wait()
    copies[3].wait()
    for a in range(blocks):
        total = matmul(lap[a, :, :cycle], jnp.concatenate(ring_rows(value, a), axis=0))
        total = total + matmul(lap[a, :, cycle + pixels:], value[rows_ref[1, a]])
        part[a] = total * keep[a].astype(F32)
    for pairing, send in zip(ORDER, sends):
        heading = send_heading(pairing, device)
        for s in range(slots):
            b = lists_ref[0, s, heading]
            base = s * 2 * pixels
            send[base:base + pixels, :] = value[b] + (1 - keep[b]) * OUTSIDE
            send[base + pixels:base + 2 * pixels, :] = part[b].astype(BF16)


def early_kernel(
    feat_ref, cot_ref, lap, value, weight_hbm, bias_hbm,
    turned, zero_sums, mix, mix_last, bias_row,
    weight, bias, sem,
):
    blocks, pixels, lanes = feat_ref.shape
    cycle = len(CYCLE_STEPS) * pixels
    copies = [
        pltpu.make_async_copy(weight_hbm, weight, sem.at[0]),
        pltpu.make_async_copy(bias_hbm, bias, sem.at[1]),
    ]
    for copy in copies:
        copy.start()
    for a in range(blocks):
        turned[a] = matmul_tn(lap[a, :, cycle:cycle + pixels], value[a])
    feat = feat_ref[...].reshape(blocks * pixels, lanes)
    cot = cot_ref[...].reshape(blocks * pixels, lanes)
    zero_sums[:lanes, :] = matmul_tn(feat, cot)
    zero_sums[lanes:, :] = jnp.broadcast_to(
        jnp.sum(cot.astype(F32), axis=0, keepdims=True), (8, lanes)
    )
    for copy in copies:
        copy.wait()
    terms, half, _ = weight.shape
    mix[...] = jnp.zeros_like(mix)
    mix_last[...] = jnp.zeros_like(mix_last)
    for m in range(lanes // half):
        spot = slice(m * half, (m + 1) * half)
        for k in range(terms - 1):
            shifted = slice(k * lanes + m * half, k * lanes + (m + 1) * half)
            mix[spot, shifted] = weight[k]
        mix_last[spot, spot] = weight[terms - 1]
        bias_row[:, spot] = bias[...]


def middle_kernel(
    rows_ref, lists_ref, feat_ref, cot_ref, lap, keep, part, turned, zero_sums, *refs,
):
    gots, (one, two, spread), sends, (sums,) = refs[:4], refs[4:7], refs[7:11], refs[11:12]
    halo, halo_part, keep_far = refs[12:]
    blocks, pixels, lanes = feat_ref.shape
    slots = lists_ref.shape[1]
    cycle = len(CYCLE_STEPS) * pixels
    flat, width = blocks * pixels, 2 * lanes
    device = lax.axis_index("pix")
    for pairing, got in zip(ORDER, gots):
        heading = send_heading(pairing, device) ^ 1
        for s in range(slots):
            row = row_of_slot(rows_ref, heading * slots + s)
            base = s * 2 * pixels
            arrived = got[base:base + pixels, :].astype(F32)
            outside = arrived > OUTSIDE / 2
            halo[row] = jnp.where(outside, 0.0, arrived).astype(BF16)
            keep_far[row] = jnp.where(outside, 0.0, 1.0).astype(BF16)
            halo_part[row] = got[base + pixels:base + 2 * pixels, :]
    for a in range(blocks):
        cross = lap[a, :, cycle:cycle + pixels]
        total = part[a] + matmul(cross, halo[a]) * keep[a].astype(F32)
        one[a] = total.astype(BF16)
        total = halo_part[a].astype(F32) + turned[a] * keep_far[a].astype(F32)
        halo[a] = total.astype(BF16)
    for a in range(blocks):
        near = ring_rows(one, a) + [halo[a], one[rows_ref[1, a]]]
        total = matmul(lap[a], jnp.concatenate(near, axis=0)) * keep[a].astype(F32)
        base = jnp.concatenate([feat_ref[a], cot_ref[a]], axis=1).astype(F32)
        fresh = (2.0 * total - base).astype(BF16)
        two[a] = fresh
        spread[a] = fresh * keep[a]
    for pairing, send in zip(ORDER_TWO, sends):
        heading = send_heading(pairing, device)
        for s in range(slots):
            send[s * pixels:(s + 1) * pixels, :] = spread[lists_ref[0, s, heading]]
    cot = cot_ref[...].reshape(flat, lanes)
    first = one[...].reshape(flat, width)
    second = two[...].reshape(flat, width)
    half = lanes // 2
    low = matmul_tn(first[:, :lanes], cot)
    high = matmul_tn(
        jnp.concatenate([first[:, :lanes], second[:, :lanes]], axis=1), first[:, lanes:]
    )

    def trace(product, start):
        return (
            product[start:start + half, :half] + product[start + half:start + lanes, half:]
        )

    sum_zero = trace(zero_sums, 0)
    sum_one = trace(low, 0)
    totals = jnp.concatenate(
        [
            jnp.concatenate([sum_zero, sum_one], axis=1),
            jnp.concatenate(
                [2.0 * trace(high, 0) - sum_zero, 2.0 * trace(high, lanes) - sum_one], axis=1
            ),
            zero_sums[lanes:, :],
        ],
        axis=0,
    )
    sums[...] = totals


def partial_kernel(
    rows_ref, feat_ref, cot_ref, lap, keep, one, two, spread, mix, bias_row,
    out_part, grad_part, three_part,
):
    blocks, pixels, lanes = feat_ref.shape
    cycle = len(CYCLE_STEPS) * pixels
    for a in range(blocks):
        total = matmul(lap[a, :, :cycle], jnp.concatenate(ring_rows(spread, a), axis=0))
        total = total + matmul(lap[a, :, cycle + pixels:], spread[rows_ref[1, a]])
        three_part[a] = 2.0 * total * keep[a].astype(F32) - one[a].astype(F32)
    flat = blocks * pixels
    first = one[...].reshape(flat, 2 * lanes)
    second = two[...].reshape(flat, 2 * lanes)
    total = jnp.broadcast_to(bias_row[...], (flat, lanes))
    fields = [feat_ref[...].reshape(flat, lanes), first[:, :lanes], second[:, :lanes]]
    for k, field in enumerate(fields):
        total = total + matmul(field, mix[:, k * lanes:(k + 1) * lanes])
    out_part[...] = total.reshape(blocks, pixels, lanes)
    fields = [cot_ref[...].reshape(flat, lanes), first[:, lanes:], second[:, lanes:]]
    total = matmul_nt(jnp.concatenate(fields, axis=1), mix[...])
    grad_part[...] = total.reshape(blocks, pixels, lanes)


def last_kernel(
    rows_ref, lap, keep, out_part, grad_part, three_part, mix_last, *refs,
):
    gots, (out_hbm, grad_hbm), (halo, three, out_ref, grad_ref, sem) = refs[:4], refs[4:6], refs[6:]
    blocks, pixels, lanes = out_part.shape
    device = lax.axis_index("pix")
    slots = gots[0].shape[0] // pixels
    for pairing, got in zip(ORDER_TWO, gots):
        heading = send_heading(pairing, device) ^ 1
        for s in range(slots):
            row = row_of_slot(rows_ref, heading * slots + s)
            halo[row] = got[s * pixels:(s + 1) * pixels, :]
    cycle = len(CYCLE_STEPS) * pixels
    group = blocks // SPLIT
    size = group * pixels
    copies = []
    for start in range(0, blocks, group):
        for a in range(start, start + group):
            total = matmul(lap[a, :, cycle:cycle + pixels], halo[a]) * keep[a].astype(F32)
            three[a] = (three_part[a] + 2.0 * total).astype(BF16)
        mine = pl.ds(start, group)
        last = three[mine].reshape(size, 2 * lanes)
        total = out_part[mine].reshape(size, lanes) + matmul(last[:, :lanes], mix_last[...])
        out_ref[mine] = total.astype(BF16).reshape(group, pixels, lanes)
        total = grad_part[mine].reshape(size, lanes) + matmul_nt(last[:, lanes:], mix_last[...])
        grad_ref[mine] = total.astype(BF16).reshape(group, pixels, lanes)
        for source, target in ((out_ref, out_hbm), (grad_ref, grad_hbm)):
            copies.append(
                pltpu.make_async_copy(source.at[mine], target.at[mine], sem.at[len(copies)])
            )
            copies[-1].start()
    for copy in copies:
        copy.wait()


def finish_kernel(factor, mine, other, weight_ref, bias_ref):
    sums = (mine[...] + other[...]) * factor
    terms, half, _ = weight_ref.shape
    lanes = 2 * half
    for k in range(terms):
        rows, cols = k // 2 * half, k % 2 * half
        weight_ref[k] = sums[rows:rows + half, cols:cols + half]
    bias = sums[lanes:lanes + 1, :]
    bias_ref[...] = bias[:, :half] + bias[:, half:]


def call(kernel, outs, ins, scratch, flops, hbm_from=None, out_hbm=False):
    vmem = pl.BlockSpec(memory_space=pltpu.VMEM)
    smem = pl.BlockSpec(memory_space=pltpu.SMEM)
    hbm = pl.BlockSpec(memory_space=pltpu.MemorySpace.HBM)
    touched = sum(math.prod(x.shape) * x.dtype.itemsize for x in [*ins, *outs])
    hbm_from = len(ins) if hbm_from is None else hbm_from
    ins = ins[:hbm_from] + [
        pltpu.with_memory_space_constraint(x, pltpu.MemorySpace.HBM) for x in ins[hbm_from:]
    ]

    def place(i, x):
        if i >= hbm_from:
            return hbm
        return smem if i < 2 and x.dtype == jnp.int32 else vmem

    return pl.pallas_call(
        kernel,
        out_shape=outs,
        in_specs=[place(i, x) for i, x in enumerate(ins)],
        out_specs=[hbm if out_hbm else smem if x.dtype == jnp.int32 else vmem for x in outs],
        scratch_shapes=scratch,
        cost_estimate=pl.CostEstimate(flops=flops, transcendentals=0, bytes_accessed=touched),
        compiler_params=pltpu.CompilerParams(vmem_limit_bytes=32 << 20),
    )(*ins)


def local(
    features, cheb_weights, out_bias, lap_tiles, neighbours, send_blocks, pixel_mask, cotangent
):
    blocks, pixels, lanes = features.shape
    terms, chan_in, chan_out = cheb_weights.shape
    slots = send_blocks.shape[2]
    width, flat = 2 * lanes, blocks * pixels
    shape = jax.ShapeDtypeStruct
    apply_flops = 2 * flat * width * lap_tiles.shape[2]
    rows = neighbours.T
    lists = send_blocks.transpose(0, 2, 1)

    field = shape((blocks, pixels, width), BF16)
    wide = shape((blocks, pixels, width), F32)
    scratch_field = pltpu.VMEM((blocks, pixels, width), BF16)
    *sends, value, keep, part, rows, lists = call(
        pack_kernel,
        [shape((slots * 2 * pixels, width), BF16)] * 4 + [field, field, wide]
        + [shape(rows.shape, jnp.int32), shape(lists.shape, jnp.int32)],
        [rows, lists, pixel_mask, features, cotangent, lap_tiles],
        [
            pltpu.VMEM((blocks, pixels), jnp.int32),
            pltpu.VMEM(lap_tiles.shape, BF16),
            pltpu.SemaphoreType.DMA((6,)),
        ],
        apply_flops,
        hbm_from=0,
    )
    gots = [exchange(send, k) for k, send in zip(ORDER, sends)]
    *early, mix, mix_last, bias_row = call(
        early_kernel,
        [wide, shape((lanes + 8, lanes), F32)]
        + [shape((lanes, (terms - 1) * lanes), BF16), shape((lanes, lanes), BF16)]
        + [shape((1, lanes), F32)],
        [features, cotangent, lap_tiles, value, cheb_weights, out_bias.reshape(1, chan_out)],
        [
            pltpu.VMEM(cheb_weights.shape, BF16),
            pltpu.VMEM((1, chan_out), F32),
            pltpu.SemaphoreType.DMA((2,)),
        ],
        2 * flat * (width * pixels + lanes * lanes),
        hbm_from=4,
    )
    one, two, spread, *sends, sums = call(
        middle_kernel,
        [field, field, field]
        + [shape((slots * pixels, width), BF16)] * 4
        + [shape((lanes + 8, lanes), F32)],
        [rows, lists, features, cotangent, lap_tiles, keep, part, *early, *gots],
        [scratch_field, scratch_field, scratch_field],
        2 * apply_flops,
    )
    gots = [exchange(send, k) for k, send in zip(ORDER_TWO, sends)]
    half_field = shape((blocks, pixels, lanes), F32)
    parts = call(
        partial_kernel,
        [half_field, half_field, wide],
        [rows, features, cotangent, lap_tiles, keep, one, two, spread]
        + [mix, bias_row],
        [],
        apply_flops + 4 * flat * lanes * lanes * (terms - 1),
    )
    count = lax.axis_size("pix")
    pair = lax.axis_size("dp")
    factor = 1.0 / math.sqrt(flat * (lanes // chan_in) * count * pair)

    def swap(block, reach):
        return lax.ppermute(block, "pix", [(i ^ reach, i) for i in range(count)])

    beside = lax.ppermute(sums, "dp", [(i ^ 1, i) for i in range(pair)])
    across = lax.ppermute(
        sums, ("pix", "dp"), [(i ^ (pair + 1), i) for i in range(count * pair)]
    )
    other = swap(sums, 1) + across
    sums = sums + beside
    reach = 2
    while reach < count:
        sums = sums + other
        other = swap(sums, reach)
        reach *= 2
    output_maps, grad_features = call(
        last_kernel,
        [shape(features.shape, BF16), shape(features.shape, BF16)],
        [rows, lap_tiles, keep, *parts, mix_last, *gots],
        [scratch_field, scratch_field]
        + [pltpu.VMEM(features.shape, BF16)] * 2
        + [pltpu.SemaphoreType.DMA((2 * SPLIT,))],
        apply_flops,
        out_hbm=True,
    )
    grad_weights, grad_bias = call(
        functools.partial(finish_kernel, factor),
        [shape(cheb_weights.shape, F32), shape((1, chan_out), F32)],
        [sums, other],
        [],
        sums.size,
    )
    return output_maps, grad_features, grad_weights, grad_bias.reshape(chan_out)


def solution(mesh):
    return jax.shard_map(
        local,
        mesh=mesh,
        in_specs=(
            P("pix", None, ("groups", "dp")),
            P(),
            P(),
            P("pix", None, None),
            P("pix", None),
            P("pix", None, None),
            P("pix", None),
            P("pix", None, ("groups", "dp")),
        ),
        out_specs=(
            P("pix", None, ("groups", "dp")),
            P("pix", None, ("groups", "dp")),
            P("groups", None, None),
            P("groups"),
        ),
        check_vma=False,
    )
```

```python
import functools
import math

import jax
import jax.numpy as jnp
from jax import lax
from jax.experimental import pallas as pl
from jax.experimental.pallas import tpu as pltpu
from jax.sharding import PartitionSpec as P

CYCLE_STEPS = (0, -1, 1, -2, 2, -3, 3)
ORDER = (3, 1, 2, 0)
ORDER_TWO = (3, 1, 2, 0)
SPLIT = 1
OUTSIDE = 16
F32 = jnp.float32
BF16 = jnp.bfloat16


def pair_of(index, pairing, count):
    if pairing == 0:
        return index ^ 1
    if pairing == 1:
        return (index + 1 if index % 2 else index - 1) % count
    low = index % 4 < 2
    step = 2 if low == (pairing == 2) else -2
    return (index + step) % count


def exchange(block, pairing):
    count = lax.axis_size("pix")
    route = [(pair_of(i, pairing, count), i) for i in range(count)]
    return lax.ppermute(block, "pix", route)


def send_heading(pairing, device):
    if pairing < 2:
        return (device + pairing) % 2
    return 2 + (device // 2 + pairing) % 2


def matmul(left, right):
    return jnp.dot(left, right, preferred_element_type=F32)


def matmul_tn(left, right):
    return lax.dot_general(left, right, (((0,), (0,)), ((), ())), preferred_element_type=F32)


def matmul_nt(left, right):
    return lax.dot_general(left, right, (((1,), (1,)), ((), ())), preferred_element_type=F32)


def row_of_slot(rows_ref, slot):
    blocks = rows_ref.shape[1]
    found = jnp.int32(0)
    for a in range(blocks):
        found = jnp.where(rows_ref[0, a] == blocks + slot, a, found)
    return found


def ring_rows(field, a):
    blocks = field.shape[0]
    return [field[(a + step) % blocks] for step in CYCLE_STEPS]


def pack_kernel(
    rows_hbm, lists_hbm, mask_hbm, feat_hbm, cot_hbm, lap_hbm,
    *refs,
):
    sends, (value, keep, part, rows_ref, lists_ref) = refs[:4], refs[4:9]
    mask, lap, sem = refs[9:]
    blocks, pixels, lanes = feat_hbm.shape
    slots = lists_hbm.shape[1]
    cycle = len(CYCLE_STEPS) * pixels
    device = lax.axis_index("pix")
    copies = [
        pltpu.make_async_copy(mask_hbm, mask, sem.at[0]),
        pltpu.make_async_copy(feat_hbm, value.at[:, :, pl.ds(0, lanes)], sem.at[1]),
        pltpu.make_async_copy(cot_hbm, value.at[:, :, pl.ds(lanes, lanes)], sem.at[2]),
        pltpu.make_async_copy(lap_hbm, lap, sem.at[3]),
        pltpu.make_async_copy(rows_hbm, rows_ref, sem.at[4]),
        pltpu.make_async_copy(lists_hbm, lists_ref, sem.at[5]),
    ]
    for first in (3, 0, 1, 2, 4, 5):
        copies[first].start()
    diagonal = lax.broadcasted_iota(jnp.int32, (pixels, pixels), 0) == lax.broadcasted_iota(
        jnp.int32, (pixels, pixels), 1
    )
    copies[0].wait()
    for a in range(blocks):
        row = mask[a:a + 1, :].astype(F32)
        column = jnp.sum(jnp.where(diagonal, row, 0.0), axis=1, keepdims=True)
        keep[a] = jnp.broadcast_to(column, (pixels, 2 * lanes)).astype(BF16)
    copies[1].wait()
    copies[2].wait()
    masked = [value[a] * keep[a] for a in range(blocks)]
    for a in range(blocks):
        value[a] = masked[a]
    copies[4].wait()
    copies[5].wait()
    copies[3].wait()
    for a in range(blocks):
        total = matmul(lap[a, :, :cycle], jnp.concatenate(ring_rows(value, a), axis=0))
        total = total + matmul(lap[a, :, cycle + pixels:], value[rows_ref[1, a]])
        part[a] = total * keep[a].astype(F32)
    for pairing, send in zip(ORDER, sends):
        heading = send_heading(pairing, device)
        for s in range(slots):
            b = lists_ref[0, s, heading]
            base = s * 2 * pixels
            send[base:base + pixels, :] = value[b] + (1 - keep[b]) * OUTSIDE
            send[base + pixels:base + 2 * pixels, :] = part[b].astype(BF16)


def early_kernel(
    feat_ref, cot_ref, lap, value, weight_hbm, bias_hbm,
    turned, zero_sums, mix, mix_last, bias_row,
    weight, bias, sem,
):
    blocks, pixels, lanes = feat_ref.shape
    cycle = len(CYCLE_STEPS) * pixels
    copies = [
        pltpu.make_async_copy(weight_hbm, weight, sem.at[0]),
        pltpu.make_async_copy(bias_hbm, bias, sem.at[1]),
    ]
    for copy in copies:
        copy.start()
    for a in range(blocks):
        turned[a] = matmul_tn(lap[a, :, cycle:cycle + pixels], value[a])
    feat = feat_ref[...].reshape(blocks * pixels, lanes)
    cot = cot_ref[...].reshape(blocks * pixels, lanes)
    zero_sums[:lanes, :] = matmul_tn(feat, cot)
    zero_sums[lanes:, :] = jnp.broadcast_to(
        jnp.sum(cot.astype(F32), axis=0, keepdims=True), (8, lanes)
    )
    for copy in copies:
        copy.wait()
    terms, half, _ = weight.shape
    mix[...] = jnp.zeros_like(mix)
    mix_last[...] = jnp.zeros_like(mix_last)
    for m in range(lanes // half):
        spot = slice(m * half, (m + 1) * half)
        for k in range(terms - 1):
            shifted = slice(k * lanes + m * half, k * lanes + (m + 1) * half)
            mix[spot, shifted] = weight[k]
        mix_last[spot, spot] = weight[terms - 1]
        bias_row[:, spot] = bias[...]


def middle_kernel(
    rows_ref, lists_ref, feat_ref, cot_ref, lap, keep, part, turned, zero_sums, *refs,
):
    gots, (one, two, spread), sends, (sums,) = refs[:4], refs[4:7], refs[7:11], refs[11:12]
    halo, halo_part, keep_far = refs[12:]
    blocks, pixels, lanes = feat_ref.shape
    slots = lists_ref.shape[1]
    cycle = len(CYCLE_STEPS) * pixels
    flat, width = blocks * pixels, 2 * lanes
    device = lax.axis_index("pix")
    for pairing, got in zip(ORDER, gots):
        heading = send_heading(pairing, device) ^ 1
        for s in range(slots):
            row = row_of_slot(rows_ref, heading * slots + s)
            base = s * 2 * pixels
            arrived = got[base:base + pixels, :].astype(F32)
            outside = arrived > OUTSIDE / 2
            halo[row] = jnp.where(outside, 0.0, arrived).astype(BF16)
            keep_far[row] = jnp.where(outside, 0.0, 1.0).astype(BF16)
            halo_part[row] = got[base + pixels:base + 2 * pixels, :]
    for a in range(blocks):
        cross = lap[a, :, cycle:cycle + pixels]
        total = part[a] + matmul(cross, halo[a]) * keep[a].astype(F32)
        one[a] = total.astype(BF16)
        total = halo_part[a].astype(F32) + turned[a] * keep_far[a].astype(F32)
        halo[a] = total.astype(BF16)
    for a in range(blocks):
        near = ring_rows(one, a) + [halo[a], one[rows_ref[1, a]]]
        total = matmul(lap[a], jnp.concatenate(near, axis=0)) * keep[a].astype(F32)
        base = jnp.concatenate([feat_ref[a], cot_ref[a]], axis=1).astype(F32)
        fresh = (2.0 * total - base).astype(BF16)
        two[a] = fresh
        spread[a] = fresh * keep[a]
    for pairing, send in zip(ORDER_TWO, sends):
        heading = send_heading(pairing, device)
        for s in range(slots):
            send[s * pixels:(s + 1) * pixels, :] = spread[lists_ref[0, s, heading]]
    cot = cot_ref[...].reshape(flat, lanes)
    first = one[...].reshape(flat, width)
    second = two[...].reshape(flat, width)
    half = lanes // 2
    low = matmul_tn(first[:, :lanes], cot)
    high = matmul_tn(
        jnp.concatenate([first[:, :lanes], second[:, :lanes]], axis=1), first[:, lanes:]
    )

    def trace(product, start):
        return (
            product[start:start + half, :half] + product[start + half:start + lanes, half:]
        )

    sum_zero = trace(zero_sums, 0)
    sum_one = trace(low, 0)
    totals = jnp.concatenate(
        [
            jnp.concatenate([sum_zero, sum_one], axis=1),
            jnp.concatenate(
                [2.0 * trace(high, 0) - sum_zero, 2.0 * trace(high, lanes) - sum_one], axis=1
            ),
            zero_sums[lanes:, :],
        ],
        axis=0,
    )
    sums[...] = totals


def partial_kernel(
    rows_ref, feat_ref, cot_ref, lap, keep, one, two, spread, mix, bias_row,
    out_part, grad_part, three_part,
):
    blocks, pixels, lanes = feat_ref.shape
    cycle = len(CYCLE_STEPS) * pixels
    for a in range(blocks):
        total = matmul(lap[a, :, :cycle], jnp.concatenate(ring_rows(spread, a), axis=0))
        total = total + matmul(lap[a, :, cycle + pixels:], spread[rows_ref[1, a]])
        three_part[a] = 2.0 * total * keep[a].astype(F32) - one[a].astype(F32)
    flat = blocks * pixels
    first = one[...].reshape(flat, 2 * lanes)
    second = two[...].reshape(flat, 2 * lanes)
    total = jnp.broadcast_to(bias_row[...], (flat, lanes))
    fields = [feat_ref[...].reshape(flat, lanes), first[:, :lanes], second[:, :lanes]]
    for k, field in enumerate(fields):
        total = total + matmul(field, mix[:, k * lanes:(k + 1) * lanes])
    out_part[...] = total.reshape(blocks, pixels, lanes)
    fields = [cot_ref[...].reshape(flat, lanes), first[:, lanes:], second[:, lanes:]]
    total = matmul_nt(jnp.concatenate(fields, axis=1), mix[...])
    grad_part[...] = total.reshape(blocks, pixels, lanes)


def last_kernel(
    rows_ref, lap, keep, out_part, grad_part, three_part, mix_last, *refs,
):
    gots, (out_hbm, grad_hbm), (halo, three, out_ref, grad_ref, sem) = refs[:4], refs[4:6], refs[6:]
    blocks, pixels, lanes = out_part.shape
    device = lax.axis_index("pix")
    slots = gots[0].shape[0] // pixels
    for pairing, got in zip(ORDER_TWO, gots):
        heading = send_heading(pairing, device) ^ 1
        for s in range(slots):
            row = row_of_slot(rows_ref, heading * slots + s)
            halo[row] = got[s * pixels:(s + 1) * pixels, :]
    cycle = len(CYCLE_STEPS) * pixels
    group = blocks // SPLIT
    size = group * pixels
    copies = []
    for start in range(0, blocks, group):
        for a in range(start, start + group):
            total = matmul(lap[a, :, cycle:cycle + pixels], halo[a]) * keep[a].astype(F32)
            three[a] = (three_part[a] + 2.0 * total).astype(BF16)
        mine = pl.ds(start, group)
        last = three[mine].reshape(size, 2 * lanes)
        total = out_part[mine].reshape(size, lanes) + matmul(last[:, :lanes], mix_last[...])
        out_ref[mine] = total.astype(BF16).reshape(group, pixels, lanes)
        total = grad_part[mine].reshape(size, lanes) + matmul_nt(last[:, lanes:], mix_last[...])
        grad_ref[mine] = total.astype(BF16).reshape(group, pixels, lanes)
        for source, target in ((out_ref, out_hbm), (grad_ref, grad_hbm)):
            copies.append(
                pltpu.make_async_copy(source.at[mine], target.at[mine], sem.at[len(copies)])
            )
            copies[-1].start()
    for copy in copies:
        copy.wait()


def finish_kernel(factor, mine, other, weight_ref, bias_ref):
    sums = (mine[...] + other[...]) * factor
    terms, half, _ = weight_ref.shape
    lanes = 2 * half
    for k in range(terms):
        rows, cols = k // 2 * half, k % 2 * half
        weight_ref[k] = sums[rows:rows + half, cols:cols + half]
    bias = sums[lanes:lanes + 1, :]
    bias_ref[...] = bias[:, :half] + bias[:, half:]


def call(kernel, outs, ins, scratch, flops, hbm_from=None, out_hbm=False):
    vmem = pl.BlockSpec(memory_space=pltpu.VMEM)
    smem = pl.BlockSpec(memory_space=pltpu.SMEM)
    hbm = pl.BlockSpec(memory_space=pltpu.MemorySpace.HBM)
    touched = sum(math.prod(x.shape) * x.dtype.itemsize for x in [*ins, *outs])
    hbm_from = len(ins) if hbm_from is None else hbm_from
    ins = ins[:hbm_from] + [
        pltpu.with_memory_space_constraint(x, pltpu.MemorySpace.HBM) for x in ins[hbm_from:]
    ]

    def place(i, x):
        if i >= hbm_from:
            return hbm
        return smem if i < 2 and x.dtype == jnp.int32 else vmem

    return pl.pallas_call(
        kernel,
        out_shape=outs,
        in_specs=[place(i, x) for i, x in enumerate(ins)],
        out_specs=[hbm if out_hbm else smem if x.dtype == jnp.int32 else vmem for x in outs],
        scratch_shapes=scratch,
        cost_estimate=pl.CostEstimate(flops=flops, transcendentals=0, bytes_accessed=touched),
        compiler_params=pltpu.CompilerParams(vmem_limit_bytes=32 << 20),
    )(*ins)


def local(
    features, cheb_weights, out_bias, lap_tiles, neighbours, send_blocks, pixel_mask, cotangent
):
    blocks, pixels, lanes = features.shape
    terms, chan_in, chan_out = cheb_weights.shape
    slots = send_blocks.shape[2]
    width, flat = 2 * lanes, blocks * pixels
    shape = jax.ShapeDtypeStruct
    apply_flops = 2 * flat * width * lap_tiles.shape[2]
    rows = neighbours.T
    lists = send_blocks.transpose(0, 2, 1)

    field = shape((blocks, pixels, width), BF16)
    wide = shape((blocks, pixels, width), F32)
    scratch_field = pltpu.VMEM((blocks, pixels, width), BF16)
    *sends, value, keep, part, rows, lists = call(
        pack_kernel,
        [shape((slots * 2 * pixels, width), BF16)] * 4 + [field, field, wide]
        + [shape(rows.shape, jnp.int32), shape(lists.shape, jnp.int32)],
        [rows, lists, pixel_mask, features, cotangent, lap_tiles],
        [
            pltpu.VMEM((blocks, pixels), jnp.int32),
            pltpu.VMEM(lap_tiles.shape, BF16),
            pltpu.SemaphoreType.DMA((6,)),
        ],
        apply_flops,
        hbm_from=0,
    )
    gots = [exchange(send, k) for k, send in zip(ORDER, sends)]
    *early, mix, mix_last, bias_row = call(
        early_kernel,
        [wide, shape((lanes + 8, lanes), F32)]
        + [shape((lanes, (terms - 1) * lanes), BF16), shape((lanes, lanes), BF16)]
        + [shape((1, lanes), F32)],
        [features, cotangent, lap_tiles, value, cheb_weights, out_bias.reshape(1, chan_out)],
        [
            pltpu.VMEM(cheb_weights.shape, BF16),
            pltpu.VMEM((1, chan_out), F32),
            pltpu.SemaphoreType.DMA((2,)),
        ],
        2 * flat * (width * pixels + lanes * lanes),
        hbm_from=4,
    )
    one, two, spread, *sends, sums = call(
        middle_kernel,
        [field, field, field]
        + [shape((slots * pixels, width), BF16)] * 4
        + [shape((lanes + 8, lanes), F32)],
        [rows, lists, features, cotangent, lap_tiles, keep, part, *early, *gots],
        [scratch_field, scratch_field, scratch_field],
        2 * apply_flops,
    )
    gots = [exchange(send, k) for k, send in zip(ORDER_TWO, sends)]
    half_field = shape((blocks, pixels, lanes), F32)
    parts = call(
        partial_kernel,
        [half_field, half_field, wide],
        [rows, features, cotangent, lap_tiles, keep, one, two, spread]
        + [mix, bias_row],
        [],
        apply_flops + 4 * flat * lanes * lanes * (terms - 1),
    )
    count = lax.axis_size("pix")
    pair = lax.axis_size("dp")
    factor = 1.0 / math.sqrt(flat * (lanes // chan_in) * count * pair)

    def swap(block, reach):
        return lax.ppermute(block, "pix", [(i ^ reach, i) for i in range(count)])

    beside = lax.ppermute(sums, "dp", [(i ^ 1, i) for i in range(pair)])
    across = lax.ppermute(
        sums, ("pix", "dp"), [(i ^ (pair + 1), i) for i in range(count * pair)]
    )
    other = swap(sums, 1) + across
    sums = sums + beside
    reach = 2
    while reach < count:
        sums = sums + other
        other = swap(sums, reach)
        reach *= 2
    output_maps, grad_features = call(
        last_kernel,
        [shape(features.shape, BF16), shape(features.shape, BF16)],
        [rows, lap_tiles, keep, *parts, mix_last, *gots],
        [scratch_field, scratch_field]
        + [pltpu.VMEM(features.shape, BF16)] * 2
        + [pltpu.SemaphoreType.DMA((2 * SPLIT,))],
        apply_flops,
        out_hbm=True,
    )
    grad_weights, grad_bias = call(
        functools.partial(finish_kernel, factor),
        [shape(cheb_weights.shape, F32), shape((1, chan_out), F32)],
        [sums, other],
        [],
        sums.size,
    )
    return output_maps, grad_features, grad_weights, grad_bias.reshape(chan_out)


def solution(mesh):
    return jax.shard_map(
        local,
        mesh=mesh,
        in_specs=(
            P("pix", None, ("groups", "dp")),
            P(),
            P(),
            P("pix", None, None),
            P("pix", None),
            P("pix", None, None),
            P("pix", None),
            P("pix", None, ("groups", "dp")),
        ),
        out_specs=(
            P("pix", None, ("groups", "dp")),
            P("pix", None, ("groups", "dp")),
            P("groups", None, None),
            P("groups"),
        ),
        check_vma=False,
    )
```
